32 devices in a mesh: facet: 8 (over z, x), stokes: 4 (over y, core).
Axes of the slice: x: 2, y: 2, z: 4, core: 2. Of those that a mesh axis runs over, the one named last changes fastest.
Arguments:
- strips: bfloat16 [4, 512, 16384], P('stokes', 'facet'), may hold values from -6 to 6
- sub_u: int32 [16], replicated, may hold values from 0 to 511
- counts: int32 [16], P('facet'), may hold values from 1 to 64, 512 in all
- uvw: int32 [3, 16, 8192], P(None, 'facet'), may hold values from 0 to 255
- mueller: float32 [4, 4, 16, 64], P(None, None, 'facet'), may hold values from -3 to 3
- observed: float32 [4, 16, 2, 8192], P('stokes', 'facet'), may hold values from -6 to 6
Outputs:
- image_out: bfloat16 [4, 512, 16384], P('stokes', 'facet')
- residual_vis: float32 [4, 16, 2, 8192], P('stokes', 'facet')
The draws below stay inside these ranges and needn't reach their ends.
Inputs may be any that keep to these rules, and one draw needn't show every extreme that they name: Block counts of one subgrid are at most 64; some subgrid has exactly 64.
All inputs are finite; a program needn't handle non-finite values.
Results may differ from the reference program's by a relative error of at most 0.018.
Values may be sent and summed in bfloat16 or wider, within the bound.
A program may use at most 128 MiB of HBM per device.

```python
import math
import jax
import jax.numpy as jnp
import numpy as np
from jax import lax

RF = 64
L = 8192
K = 64
G = 256
MAXB = 64
BLOCK = 128
VISITS = 8192
NSUB = 16
NR = 512
N_FACET = 8


def set_ends(values, key, least, high):
    place = [jax.random.randint(jax.random.fold_in(key, axis), (), 0, length) for axis, length in enumerate(values.shape)]
    main_axis = values.shape.index(max(values.shape))
    beside = place[:main_axis] + [(place[main_axis] + 1) % values.shape[main_axis]] + place[main_axis + 1:]
    return values.at[tuple(place)].set(least).at[tuple(beside)].set(high)


def steps_of(rng, shape, cuts, smallest, high):
    loudness, own = 1.0, jax.random.fold_in(rng, 6)
    for dim, parts in cuts:
        draws = jnp.exp(jax.random.uniform(jax.random.fold_in(own, dim), (parts,), jnp.float32, smallest / len(cuts), high / len(cuts)))
        loudness = loudness * jnp.repeat(draws, shape[dim] // parts).reshape([-1 if axis == dim else 1 for axis in range(len(shape))])
    return loudness


def profile(amount, total, reach, lean):
    weights = [(1 << 20) // math.isqrt(rank ** lean) + 1 for rank in range(2, amount + 1)]
    surplus, given = total - reach - (amount - 1), [1] * (amount - 1)
    while surplus > 0:
        free = [i for i in range(amount - 1) if given[i] < reach]
        mass, remaining = sum([weights[i] for i in free]), surplus
        for i in free:
            addition = min(reach - given[i], max(1, remaining * weights[i] // mass), surplus)
            given[i] = given[i] + addition
            surplus = surplus - addition
    return np.array([reach] + given)


def ragged(own_key, number_of, total, reach, lean):
    if number_of == 2:
        one = jax.random.randint(own_key, (), max(1, total - reach), min(reach, total - 1) + 1)
        return jnp.stack([one, total - one])
    lengths = jnp.asarray(profile(number_of, total, reach, lean), jnp.int32)
    twos = (number_of - 1) // 2
    source_of, receiver = lengths[1:1 + 2 * twos:2], lengths[2:2 + 2 * twos:2]
    margin = jnp.minimum(source_of - 1, reach - receiver)
    shifted = jax.random.randint(jax.random.fold_in(own_key, 1), (twos,), 0, 1 << 20) % (margin + 1)
    lengths = lengths.at[1:1 + 2 * twos:2].set(source_of - shifted).at[2:2 + 2 * twos:2].set(receiver + shifted)
    return lengths[jax.random.permutation(jax.random.fold_in(own_key, 2), number_of)]


def normal_values(rng, extent, deviation, bound, split=(), kind=jnp.bfloat16):
    loudness = steps_of(rng, extent, split, -0.22, 0.18) if split else 1.0
    entries = jax.random.normal(rng, extent, jnp.float32) * deviation * loudness
    return jnp.minimum(jnp.maximum(entries, -bound), bound).astype(kind)


def setup_inputs(seed: int = 0) -> dict:
    seeds = jax.random.split(jax.random.key(seed), 7)
    strips = normal_values(seeds[0], (4, NR, 2 * L), 1.0, 6.0, ((0, 4), (1, 8)))
    sub_u = set_ends(jax.random.randint(seeds[1], (NSUB,), 0, NR), jax.random.fold_in(seeds[1], 1), 0, NR - 1).astype(jnp.int32)
    counts = ragged(seeds[2], NSUB, NSUB * MAXB // 2, MAXB, 2).astype(jnp.int32)
    uvw = set_ends(jax.random.randint(seeds[3], (3, NSUB, VISITS), 0, G), jax.random.fold_in(seeds[3], 1), 0, G - 1).astype(jnp.int32)
    mueller = normal_values(seeds[4], (4, 4, NSUB, MAXB), 0.6, 3.0, ((2, 8),), jnp.float32)
    observed = normal_values(seeds[5], (4, NSUB, 2, VISITS), 1.0, 6.0, ((0, 4), (1, 8)), jnp.float32)
    return {"strips": strips, "sub_u": sub_u, "counts": counts, "uvw": uvw, "mueller": mueller, "observed": observed}


full_turn = 2.0 * math.pi

def turn(phase, period):
    angle = phase.astype(jnp.float32) * (full_turn / period)
    return (jnp.cos(angle), jnp.sin(angle))

def lower(value):
    return lax.optimization_barrier(value.astype(jnp.bfloat16))

def stack_right(real, imag):
    return jnp.concatenate([jnp.concatenate([real, imag], 1), jnp.concatenate([-imag, real], 1)], 0)

def column_table(length, samples):
    lpos = jnp.arange(length, dtype=jnp.int32)[:, None]
    cpos = jnp.arange(samples, dtype=jnp.int32)[None, :]
    cosine, sine = turn(4 * cpos * lpos % length, length)
    scale = 1.0 / math.sqrt(length)
    return stack_right(cosine * scale, -sine * scale).astype(jnp.bfloat16)

def interp_table(width, samples):
    upos = jnp.arange(width, dtype=jnp.int32)[:, None, None]
    kpos = jnp.arange(samples, dtype=jnp.int32)[None, :, None]
    mpos = jnp.arange(samples, dtype=jnp.int32)[None, None, :] - samples // 2
    cosine, sine = turn(jnp.remainder(mpos * (upos - 4 * kpos), width), width)
    return (lax.optimization_barrier(jnp.sum(cosine, 2)) / (2.0 * samples), lax.optimization_barrier(jnp.sum(sine, 2)) / (2.0 * samples))

def facet_table(real, imag, facets, rows, total):
    width, samples = real.shape
    centre = (facets * rows + rows // 2)[None, :, None]
    upos = jnp.arange(width, dtype=jnp.int32)[:, None, None]
    kpos = jnp.arange(samples, dtype=jnp.int32)[None, None, :]
    phase = 4 * kpos * centre % total - upos * centre % total
    cosine, sine = turn(phase, total)
    e_real = real[:, None, :] * cosine - imag[:, None, :] * sine
    e_imag = real[:, None, :] * sine + imag[:, None, :] * cosine
    return (e_real, e_imag)

def row_table(offsets, positions, total, samples):
    kpos = jnp.arange(samples, dtype=jnp.int32)
    freq = (offsets[:, None] + 4 * kpos[None, :]) % total
    phase = freq[:, :, None] * positions[None, None, :] % total
    cosine, sine = turn(phase, total)
    scale = 1.0 / math.sqrt(total)
    return (cosine * scale, -sine * scale)

def join(first, second, conj):
    half = first.shape[-1] // 2
    if conj:
        real = first[..., :half] + second[..., half:]
        imag = first[..., half:] - second[..., :half]
    else:
        real = first[..., :half] - second[..., half:]
        imag = first[..., half:] + second[..., :half]
    return jnp.concatenate([real, imag], -1)

def cein(form, left_re, left_im, packed, conj):
    hp = lax.Precision.HIGHEST
    right = packed.astype(jnp.float32)
    first = jnp.einsum(form, left_re.astype(jnp.float32), right, precision=hp)
    second = jnp.einsum(form, left_im.astype(jnp.float32), right, precision=hp)
    return join(first, second, conj)

def reference(strips, sub_u, counts, uvw, mueller, observed):
    total = RF * N_FACET
    hp = lax.Precision.HIGHEST
    column = column_table(L, K)
    coeffs = lower(jnp.dot(strips, column, preferred_element_type=jnp.float32))
    blocked = coeffs.reshape(4, N_FACET, RF, 2 * K)
    b_re, b_im = interp_table(G, K)
    e_re, e_im = facet_table(b_re, b_im, jnp.arange(N_FACET, dtype=jnp.int32), RF, total)
    e_re = lower(e_re)
    e_im = lower(e_im)
    lb_re = lower(b_re).astype(jnp.float32)
    lb_im = lower(b_im).astype(jnp.float32)
    s_tab = stack_right(lb_re.T, lb_im.T)
    positions = jnp.arange(total, dtype=jnp.int32)
    blocks = jnp.arange(MAXB, dtype=jnp.int32)

    def one_subgrid(carry, items):
        offset, count, coords, mix, seen = items
        r_re, r_im = row_table(offset[None], positions, total, K)
        r_re = lower(r_re.reshape(K, N_FACET, RF))
        r_im = lower(r_im.reshape(K, N_FACET, RF))
        patches = lower(cein('kfr,sfrc->sfkc', r_re, r_im, blocked, False))
        lifted = lower(cein('ufk,sfkc->suc', e_re, e_im, patches, False))
        subgrid = jnp.einsum('sux,xy->suy', lifted.astype(jnp.float32), s_tab, precision=hp)
        flat = subgrid.reshape(4, G * 2 * G)
        index = (coords[0] * (2 * G) + coords[1]).astype(jnp.int32)
        m_re = flat[:, index]
        m_im = flat[:, index + G]
        cosine, sine = turn(coords[2], G)
        mod_re = m_re * cosine + m_im * sine
        mod_im = m_im * cosine - m_re * sine
        model = jnp.stack([mod_re, mod_im], 1).reshape(4, 2, MAXB, BLOCK)
        corr = lax.optimization_barrier(jnp.sum(mix[:, :, None, :, None] * model[None], axis=1))
        live = (blocks < count).astype(jnp.float32)[None, None, :, None]
        resid = (seen.reshape(4, 2, MAXB, BLOCK) - corr) * live
        back = lax.optimization_barrier(jnp.sum(mix[:, :, None, :, None] * resid[:, None], axis=0)).reshape(4, 2, VISITS)
        g_re = back[:, 0] * cosine - back[:, 1] * sine
        g_im = back[:, 1] * cosine + back[:, 0] * sine
        w_re = lb_re[coords[1]][None]
        w_im = lb_im[coords[1]][None]
        v_re = g_re[..., None] * w_re + g_im[..., None] * w_im
        v_im = g_im[..., None] * w_re - g_re[..., None] * w_im
        terms = lower(jnp.concatenate([v_re, v_im], -1)).astype(jnp.float32)
        lifted_adj = lower(jnp.zeros((4, G, 2 * K), jnp.float32).at[:, coords[0]].add(terms))
        patches_adj = lower(cein('ufk,suc->sfkc', e_re, e_im, lifted_adj, True))
        contrib = cein('kfr,sfkc->sfrc', r_re, r_im, patches_adj, True)
        return (carry + contrib.reshape(4, total, 2 * K), resid.reshape(4, 2, VISITS))
    items = (sub_u, counts, jnp.transpose(uvw, (1, 0, 2)), jnp.transpose(mueller, (2, 0, 1, 3)), jnp.transpose(observed, (1, 0, 2, 3)))
    sums, resids = lax.scan(one_subgrid, jnp.zeros((4, total, 2 * K), jnp.float32), items)
    image = lax.dot_general(sums.astype(jnp.bfloat16), column, (((2,), (1,)), ((), ())), preferred_element_type=jnp.float32)
    image_out = (8.0 * image).astype(jnp.bfloat16)
    return (image_out, jnp.transpose(resids, (1, 0, 2, 3)))
```

```python
import functools
import math

import jax
import jax.numpy as jnp
import ml_dtypes
import numpy as np
from jax import lax
from jax.experimental import pallas as pl
from jax.experimental.pallas import tpu as pltpu
from jax.sharding import PartitionSpec as P

K = 64
G = 256
BLOCK = 128
PAIR = 2 * BLOCK
MESH = pl.DeviceIdType.MESH
VMEM_BYTES = 60 * 1024 * 1024


def unit(phase, period):
    angle = phase.astype(np.float64) * (2.0 * math.pi / period)
    return np.cos(angle) + 1j * np.sin(angle)


def column_table(length):
    period = length // 4
    lpos = np.arange(period, dtype=np.int64)[:, None]
    cpos = np.arange(K, dtype=np.int64)[None, :]
    table = unit(-(4 * cpos * lpos % length), length) / math.sqrt(length)
    re, im = table.real, table.imag
    return np.concatenate([np.concatenate([re, im], 1), np.concatenate([-im, re], 1)], 0).astype(
        ml_dtypes.bfloat16
    )


def interp_table():
    upos = np.arange(G, dtype=np.int64)[:, None, None]
    kpos = np.arange(K, dtype=np.int64)[None, :, None]
    mpos = np.arange(K, dtype=np.int64)[None, None, :] - K // 2
    return unit(mpos * (upos - 4 * kpos) % G, G).sum(2) / (2.0 * K)


def lift_table(interp, nfac, rows):
    total = nfac * rows
    upos = np.arange(G, dtype=np.int64)[:, None]
    kpos = np.arange(K, dtype=np.int64)
    blocks = []
    for f in range(nfac):
        centre = f * rows + rows // 2
        e = interp * unit(4 * kpos[None, :] * centre % total - upos * centre % total, total)
        rpos = f * rows + np.arange(rows, dtype=np.int64)
        fourier = unit(-(4 * kpos[:, None] * rpos[None, :] % total), total) / math.sqrt(total)
        blocks.append(e @ fourier)
    return np.concatenate(blocks, 1)


def half_sign(shape, first):
    lane = lax.broadcasted_iota(jnp.int32, shape, 1)
    return jnp.where(lane < K, first, -first).astype(jnp.float32)


def entry_barrier(f, s, nfac, nst):
    barrier = pltpu.get_barrier_semaphore()
    for k in range(1, nfac):
        pl.semaphore_signal(barrier, inc=1, device_id=(lax.rem(f + k, nfac), s), device_id_type=MESH)
    for k in range(1, nst):
        pl.semaphore_signal(barrier, inc=1, device_id=(f, s ^ k), device_id_type=MESH)
    return barrier


def predict_kernel(
    nfac,
    nst,
    owned,
    strips_ref,
    column_ref,
    m0_ref,
    ph_ref,
    obs_ref,
    yall_ref,
    obuf_ref,
    cbuf,
    osend,
    orecv,
    csend,
    crecv,
    ysend,
    yrecv,
):
    f = lax.axis_index("facet")
    s = lax.axis_index("stokes")
    rows = strips_ref.shape[1]
    steps = obuf_ref.shape[1]
    barrier = entry_barrier(f, s, nfac, nst)
    period = column_ref.shape[0] // 2
    folded = []
    for half in range(2):
        acc = None
        for rep in range(4):
            piece = strips_ref[0, :, pl.ds((half * 4 + rep) * period, period)].astype(jnp.float32)
            acc = piece if acc is None else acc + piece
        folded.append(acc.astype(jnp.bfloat16))
    coeffs = jnp.dot(folded[0], column_ref[:period], preferred_element_type=jnp.float32)
    coeffs += jnp.dot(folded[1], column_ref[period:], preferred_element_type=jnp.float32)
    mine = pl.ds(pl.multiple_of(f * rows, rows), rows)
    cbuf[mine, :] = coeffs.astype(jnp.bfloat16)
    pl.semaphore_wait(barrier, nfac + nst - 2)
    coeff_copies = []
    for k in range(1, nfac):
        copy = pltpu.make_async_remote_copy(
            src_ref=cbuf.at[mine],
            dst_ref=cbuf.at[mine],
            send_sem=csend.at[k - 1],
            recv_sem=crecv.at[k - 1],
            device_id=(lax.rem(f + k, nfac), s),
            device_id_type=MESH,
        )
        copy.start()
        coeff_copies.append(copy)
    obs_copies = []
    for k in range(1, nst):
        peer = s ^ k
        for t in range(steps):
            copy = pltpu.make_async_remote_copy(
                src_ref=obs_ref.at[0, :, :, pl.ds(pl.multiple_of((nst * t + peer) * PAIR, PAIR), PAIR)],
                dst_ref=obuf_ref.at[s, t],
                send_sem=osend.at[k - 1, t],
                recv_sem=orecv.at[k - 1, t],
                device_id=(f, peer),
                device_id_type=MESH,
            )
            copy.start()
            obs_copies.append(copy)
    for t in range(steps):
        obuf_ref[s, t] = obs_ref[0, :, :, pl.ds(pl.multiple_of((nst * t + s) * PAIR, PAIR), PAIR)]
    for copy in coeff_copies:
        copy.wait_recv()
    c = cbuf[...].astype(jnp.float32)
    sign = half_sign(c.shape, -1.0)
    swapped = pltpu.roll(c, K, 1) * sign
    tops, bottoms = [], []
    for j in range(owned):
        z = c * ph_ref[:, j : j + 1] + swapped * ph_ref[:, owned + j : owned + j + 1]
        tops.append(z.astype(jnp.bfloat16))
        bottoms.append((pltpu.roll(z, K, 1) * sign).astype(jnp.bfloat16))
    zz = jnp.concatenate([jnp.concatenate(tops, 1), jnp.concatenate(bottoms, 1)], 0)
    y = jnp.dot(m0_ref[...], zz, preferred_element_type=jnp.float32)
    yall_ref[s] = y.T.astype(jnp.bfloat16)

    def send(slot, bit, index):
        copy = pltpu.make_async_remote_copy(
            src_ref=yall_ref.at[slot],
            dst_ref=yall_ref.at[slot],
            send_sem=ysend.at[index],
            recv_sem=yrecv.at[index],
            device_id=(f, s ^ bit),
            device_id_type=MESH,
        )
        copy.start()
        return copy

    far = send(s, 2, 0)
    near = send(s, 1, 1)
    far.wait_recv()
    relay = send(s ^ 2, 1, 2)
    near.wait_recv()
    relay.wait_recv()
    for copy in obs_copies:
        copy.wait()
    for copy in coeff_copies + [far, near, relay]:
        copy.wait_send()


def turn_256(n):
    quarter = (n + 32) >> 6
    angle = (n - (quarter << 6)).astype(jnp.float32) * (2.0 * math.pi / G)
    x2 = angle * angle
    sin = angle * (1.0 + x2 * (-1.0 / 6 + x2 * (1.0 / 120 + x2 * (-1.0 / 5040 + x2 / 362880.0))))
    cos = 1.0 + x2 * (-0.5 + x2 * (1.0 / 24 + x2 * (-1.0 / 720 + x2 / 40320.0)))
    odd = (quarter & 1) == 1
    base_c = jnp.where(odd, sin, cos)
    base_s = jnp.where(odd, cos, sin)
    q = quarter & 3
    cosine = jnp.where((q == 1) | (q == 2), -base_c, base_c)
    sine = jnp.where(q >= 2, -base_s, base_s)
    return cosine, sine


def visibility_kernel(
    nst, owned, counts_ref, mu_ref, yall_ref, interp_ref, uvw_ref, obs_ref, rbuf_ref, ya_ref, acc
):
    me = lax.axis_index("stokes")
    rbuf_ref[...] = jnp.zeros_like(rbuf_ref)
    acc[...] = jnp.zeros_like(acc)
    width = 2 * K
    for j in range(owned):
        count = counts_ref[j]
        pairs = (count + 1) // 2
        trips = (pairs - me + nst - 1) // nst

        def step(t, carry):
            pair = nst * t + me
            lanes = pl.ds(pl.multiple_of(pair * PAIR, PAIR), PAIR)
            cells = lax.broadcasted_iota(jnp.int32, (G, PAIR), 0)
            pick_u = jnp.where(cells == uvw_ref[0, j : j + 1, lanes], 1.0, 0.0).astype(jnp.bfloat16)
            pick_w = jnp.where(cells == uvw_ref[1, j : j + 1, lanes], 1.0, 0.0).astype(jnp.bfloat16)
            cosine, sine = turn_256(uvw_ref[2, j : j + 1, lanes])
            table = jnp.concatenate(
                [yall_ref[s, j * width : (j + 1) * width, :] for s in range(nst)], 0
            )
            picked = jnp.dot(table, pick_u, preferred_element_type=jnp.float32)
            weights = jnp.dot(interp_ref[...], pick_w, preferred_element_type=jnp.float32)
            w_re, w_im = weights[:K], weights[K:]
            model = []
            for s in range(nst):
                y_re = picked[s * width : s * width + K]
                y_im = picked[s * width + K : (s + 1) * width]
                m_re = jnp.sum(y_re * w_re - y_im * w_im, axis=0, keepdims=True)
                m_im = jnp.sum(y_re * w_im + y_im * w_re, axis=0, keepdims=True)
                model.append(
                    jnp.concatenate([m_re * cosine + m_im * sine, m_im * cosine - m_re * sine], 0)
                )
            block = 2 * pair
            second_live = jnp.where(block + 1 < count, 1.0, 0.0)
            backs = []
            resids = []
            for h in range(2):
                cut = slice(h * BLOCK, (h + 1) * BLOCK)
                mix = [[mu_ref[c, s, j, block + h] for s in range(nst)] for c in range(nst)]
                resid = []
                for c in range(nst):
                    corr = mix[c][0] * model[0][:, cut]
                    for s in range(1, nst):
                        corr += mix[c][s] * model[s][:, cut]
                    value = obs_ref[c, t, j, :, cut] - corr
                    if h == 1:
                        value = value * second_live
                    resid.append(value)
                back = []
                for s in range(nst):
                    total = mix[0][s] * resid[0]
                    for c in range(1, nst):
                        total += mix[c][s] * resid[c]
                    back.append(total)
                backs.append(back)
                resids.append(resid)
            for c in range(nst):
                rbuf_ref[c, t, j] = jnp.concatenate([resids[0][c], resids[1][c]], 1)
            terms = []
            for s in range(nst):
                back = jnp.concatenate([backs[0][s], backs[1][s]], 1)
                b_re, b_im = back[0:1], back[1:2]
                g_re = b_re * cosine - b_im * sine
                g_im = b_im * cosine + b_re * sine
                terms.append((g_re * w_re + g_im * w_im).astype(jnp.bfloat16))
                terms.append((g_im * w_re - g_re * w_im).astype(jnp.bfloat16))
            acc[j] += lax.dot_general(
                jnp.concatenate(terms, 0),
                pick_u,
                (((1,), (1,)), ((), ())),
                preferred_element_type=jnp.float32,
            )
            return carry

        lax.fori_loop(0, trips, step, 0)
        for s in range(nst):
            ya_ref[s, j * width : (j + 1) * width, :] = acc[j, s * width : (s + 1) * width, :].astype(
                jnp.bfloat16
            )


def adjoint_kernel(
    nfac,
    nst,
    owned,
    ya_ref,
    rbuf_ref,
    m2_ref,
    ph_ref,
    sums_ref,
    rout_ref,
    stage,
    ymid,
    yin,
    part,
    parts_in,
    rsend,
    rrecv,
    ysend,
    yrecv,
    psend,
    precv,
):
    f = lax.axis_index("facet")
    s = lax.axis_index("stokes")
    rows = sums_ref.shape[0]
    width = 2 * K
    barrier = entry_barrier(f, s, nfac, nst)
    pl.semaphore_wait(barrier, nfac + nst - 2)

    def send(src, dst, bit, index):
        copy = pltpu.make_async_remote_copy(
            src_ref=src,
            dst_ref=dst,
            send_sem=ysend.at[index],
            recv_sem=yrecv.at[index],
            device_id=(f, s ^ bit),
            device_id_type=MESH,
        )
        copy.start()
        return copy

    first = send(ya_ref.at[s ^ 3], stage.at[0], 1, 0)
    second = send(ya_ref.at[s ^ 1], stage.at[1], 1, 1)
    first.wait_recv()
    ymid[...] = (ya_ref[s ^ 2].astype(jnp.float32) + stage[0].astype(jnp.float32)).astype(jnp.bfloat16)
    third = send(ymid, yin, 2, 2)
    resid_copies = []
    for k in range(1, nst):
        copy = pltpu.make_async_remote_copy(
            src_ref=rbuf_ref.at[s ^ k],
            dst_ref=rout_ref.at[s],
            send_sem=rsend.at[k - 1],
            recv_sem=rrecv.at[k - 1],
            device_id=(f, s ^ k),
            device_id_type=MESH,
        )
        copy.start()
        resid_copies.append(copy)
    rout_ref[s] = rbuf_ref[s]
    second.wait_recv()
    own = ya_ref[s].astype(jnp.float32) + stage[1].astype(jnp.float32)
    third.wait_recv()
    own = own + yin[...].astype(jnp.float32)
    turned = []
    for j in range(owned):
        turned.append(own[j * width + K : (j + 1) * width])
        turned.append(-own[j * width : j * width + K])
    rhs = jnp.concatenate([own, jnp.concatenate(turned, 0)], 1).astype(jnp.bfloat16)
    u = lax.dot_general(
        m2_ref[...], rhs, (((1,), (1,)), ((), ())), preferred_element_type=jnp.float32
    )
    partial = None
    for j in range(owned):
        uj = u[:, j * width : (j + 1) * width]
        term = uj * ph_ref[:, j : j + 1] + pltpu.roll(uj, K, 1) * half_sign(uj.shape, 1.0) * ph_ref[
            :, owned + j : owned + j + 1
        ]
        partial = term if partial is None else partial + term
    part[...] = partial.astype(jnp.bfloat16)
    part_copies = []
    for k in range(1, nfac):
        peer = lax.rem(f + k, nfac)
        copy = pltpu.make_async_remote_copy(
            src_ref=part.at[pl.ds(pl.multiple_of(peer * rows, rows), rows)],
            dst_ref=parts_in.at[k - 1],
            send_sem=psend.at[k - 1],
            recv_sem=precv.at[k - 1],
            device_id=(peer, s),
            device_id_type=MESH,
        )
        copy.start()
        part_copies.append(copy)
    result = part[pl.ds(pl.multiple_of(f * rows, rows), rows), :].astype(jnp.float32)
    for k, copy in enumerate(part_copies):
        copy.wait_recv()
        result += parts_in[k].astype(jnp.float32)
    sums_ref[...] = result.astype(jnp.bfloat16)
    for copy in resid_copies:
        copy.wait()
    for copy in part_copies + [first, second, third]:
        copy.wait_send()


def image_kernel(nst, owned, sums_ref, column_ref, rout_ref, image_ref, resid_ref, buf, sems):
    chunks = 4
    period = column_ref.shape[0] // 2
    size = 2 * period // chunks
    steps = rout_ref.shape[1]
    copies = []
    for i in range(chunks):
        cols = pl.ds(i * size, size)
        image = lax.dot_general(
            sums_ref[...], column_ref[cols, :], (((1,), (1,)), ((), ())), preferred_element_type=jnp.float32
        )
        buf[:, cols] = (8.0 * image).astype(jnp.bfloat16)
        half, offset = divmod(i * size, period)
        for rep in range(4):
            copy = pltpu.make_async_copy(
                buf.at[:, cols],
                image_ref.at[0, :, pl.ds((half * 4 + rep) * period + offset, size)],
                sems.at[i, rep],
            )
            copy.start()
            copies.append(copy)
    for q in range(nst):
        for t in range(steps):
            resid_ref[0, :, :, (nst * t + q) * PAIR : (nst * t + q + 1) * PAIR] = rout_ref[q, t]
    for copy in copies:
        copy.wait()


def body(strips, sub_u, counts, uvw, mueller, observed):
    nfac = lax.axis_size("facet")
    nst = lax.axis_size("stokes")
    here = lax.axis_index("facet")
    rows = strips.shape[1]
    length = strips.shape[2] // 2
    total = rows * nfac
    owned = counts.shape[0]
    visits = uvw.shape[2]
    steps = visits // (PAIR * nst)
    wide = owned * 2 * K
    f32, bf16 = jnp.float32, jnp.bfloat16
    interp = interp_table()
    m0 = lift_table(interp, nfac, rows)
    column = jnp.asarray(column_table(length))
    interp_t = jnp.asarray(np.concatenate([interp.real.T, interp.imag.T], 0).astype(ml_dtypes.bfloat16))
    m0_wide = jnp.asarray(np.concatenate([m0.real, m0.imag], 1).astype(ml_dtypes.bfloat16))
    m0_tall = jnp.asarray(np.concatenate([m0.real.T, m0.imag.T], 1).astype(ml_dtypes.bfloat16))
    offsets = lax.dynamic_slice_in_dim(sub_u, here * owned, owned)
    phase = jnp.arange(total, dtype=jnp.int32)[:, None] * offsets[None, :] % total
    angle = phase.astype(f32) * (2.0 * math.pi / total)
    ph = jnp.concatenate([jnp.cos(angle), -jnp.sin(angle)], 1)
    vmem = pl.BlockSpec(memory_space=pltpu.VMEM)
    smem = pl.BlockSpec(memory_space=pltpu.SMEM)
    dma = pltpu.SemaphoreType.DMA

    yall, obs = pl.pallas_call(
        functools.partial(predict_kernel, nfac, nst, owned),
        out_shape=(
            jax.ShapeDtypeStruct((nst, wide, G), bf16),
            jax.ShapeDtypeStruct((nst, steps, owned, 2, PAIR), f32),
        ),
        in_specs=[vmem] * 5,
        out_specs=(vmem, vmem),
        scratch_shapes=[
            pltpu.VMEM((total, 2 * K), bf16),
            dma((nst - 1, steps)),
            dma((nst - 1, steps)),
            dma((nfac - 1,)),
            dma((nfac - 1,)),
            dma((3,)),
            dma((3,)),
        ],
        compiler_params=pltpu.CompilerParams(
            collective_id=0, has_side_effects=True, vmem_limit_bytes=VMEM_BYTES
        ),
        name="predict",
    )(strips, column, m0_wide, ph, observed)

    rbuf, ya = pl.pallas_call(
        functools.partial(visibility_kernel, nst, owned),
        out_shape=(
            jax.ShapeDtypeStruct((nst, steps, owned, 2, PAIR), f32),
            jax.ShapeDtypeStruct((nst, wide, G), bf16),
        ),
        in_specs=[smem, smem, vmem, vmem, vmem, vmem],
        out_specs=(vmem, vmem),
        scratch_shapes=[pltpu.VMEM((owned, nst * 2 * K, G), f32)],
        compiler_params=pltpu.CompilerParams(vmem_limit_bytes=VMEM_BYTES),
        name="visibility",
    )(counts, mueller, yall, interp_t, uvw, obs)

    sums, rout = pl.pallas_call(
        functools.partial(adjoint_kernel, nfac, nst, owned),
        out_shape=(
            jax.ShapeDtypeStruct((rows, 2 * K), bf16),
            jax.ShapeDtypeStruct((nst, steps, owned, 2, PAIR), f32),
        ),
        in_specs=[vmem] * 4,
        out_specs=(vmem, vmem),
        scratch_shapes=[
            pltpu.VMEM((2, wide, G), bf16),
            pltpu.VMEM((wide, G), bf16),
            pltpu.VMEM((wide, G), bf16),
            pltpu.VMEM((total, 2 * K), bf16),
            pltpu.VMEM((nfac - 1, rows, 2 * K), bf16),
            dma((nst - 1,)),
            dma((nst - 1,)),
            dma((3,)),
            dma((3,)),
            dma((nfac - 1,)),
            dma((nfac - 1,)),
        ],
        compiler_params=pltpu.CompilerParams(
            collective_id=1, has_side_effects=True, vmem_limit_bytes=VMEM_BYTES
        ),
        name="adjoint",
    )(ya, rbuf, m0_tall, ph)

    return pl.pallas_call(
        functools.partial(image_kernel, nst, owned),
        out_shape=(
            jax.ShapeDtypeStruct((1, rows, 2 * length), bf16),
            jax.ShapeDtypeStruct((1, owned, 2, visits), f32),
        ),
        in_specs=[vmem] * 3,
        out_specs=(pl.BlockSpec(memory_space=pl.ANY), vmem),
        scratch_shapes=[pltpu.VMEM((rows, length // 2), bf16), dma((4, 4))],
        compiler_params=pltpu.CompilerParams(vmem_limit_bytes=VMEM_BYTES),
        name="image",
    )(sums, column, rout)


def solution(mesh):
    placed = (
        P("stokes", "facet", None),
        P(),
        P("facet"),
        P(None, "facet", None),
        P(None, None, "facet", None),
        P("stokes", "facet", None, None),
    )
    return jax.shard_map(
        body,
        mesh=mesh,
        in_specs=placed,
        out_specs=(P("stokes", "facet", None), P("stokes", "facet", None, None)),
        check_vma=False,
    )
```

```python
import functools
import math

import jax
import jax.numpy as jnp
import ml_dtypes
import numpy as np
from jax import lax
from jax.experimental import pallas as pl
from jax.experimental.pallas import tpu as pltpu
from jax.sharding import PartitionSpec as P

K = 64
G = 256
BLOCK = 128
PAIR = 2 * BLOCK
MESH = pl.DeviceIdType.MESH


def unit(phase, period):
    angle = phase.astype(np.float64) * (2.0 * math.pi / period)
    return np.cos(angle) + 1j * np.sin(angle)


def column_table(length):
    period = length // 4
    lpos = np.arange(period, dtype=np.int64)[:, None]
    cpos = np.arange(K, dtype=np.int64)[None, :]
    table = unit(-(4 * cpos * lpos % length), length) / math.sqrt(length)
    re, im = table.real, table.imag
    return np.concatenate([np.concatenate([re, im], 1), np.concatenate([-im, re], 1)], 0).astype(
        ml_dtypes.bfloat16
    )


def interp_table():
    upos = np.arange(G, dtype=np.int64)[:, None, None]
    kpos = np.arange(K, dtype=np.int64)[None, :, None]
    mpos = np.arange(K, dtype=np.int64)[None, None, :] - K // 2
    return unit(mpos * (upos - 4 * kpos) % G, G).sum(2) / (2.0 * K)


def lift_table(interp, nfac, rows):
    total = nfac * rows
    upos = np.arange(G, dtype=np.int64)[:, None]
    kpos = np.arange(K, dtype=np.int64)
    blocks = []
    for f in range(nfac):
        centre = f * rows + rows // 2
        e = interp * unit(4 * kpos[None, :] * centre % total - upos * centre % total, total)
        rpos = f * rows + np.arange(rows, dtype=np.int64)
        fourier = unit(-(4 * kpos[:, None] * rpos[None, :] % total), total) / math.sqrt(total)
        blocks.append(e @ fourier)
    return np.concatenate(blocks, 1)


def turn_of(n, period):
    fraction = n.astype(jnp.float32) * (4.0 / period)
    quarter = (fraction + 0.5).astype(jnp.int32)
    angle = (fraction - quarter.astype(jnp.float32)) * (0.5 * math.pi)
    x2 = angle * angle
    sin = angle * (1.0 + x2 * (-1.0 / 6 + x2 * (1.0 / 120 + x2 * (-1.0 / 5040 + x2 / 362880.0))))
    cos = 1.0 + x2 * (-0.5 + x2 * (1.0 / 24 + x2 * (-1.0 / 720 + x2 / 40320.0)))
    odd = (quarter & 1) == 1
    base_c = jnp.where(odd, sin, cos)
    base_s = jnp.where(odd, cos, sin)
    q = quarter & 3
    cosine = jnp.where((q == 1) | (q == 2), -base_c, base_c)
    sine = jnp.where(q >= 2, -base_s, base_s)
    return cosine, sine


def half_sign(shape, first):
    lane = lax.broadcasted_iota(jnp.int32, shape, 1)
    return jnp.where(lane < K, first, -first).astype(jnp.float32)


def fill_phases(offsets_ref, first, owned, ph):
    total = ph.shape[1]
    rpos = lax.broadcasted_iota(jnp.int32, ph.shape[1:], 0)
    for j in range(owned):
        product = rpos * offsets_ref[first + j]
        phase = product & (total - 1) if total & (total - 1) == 0 else lax.rem(product, total)
        cosine, sine = turn_of(phase, total)
        ph[j] = cosine
        ph[owned + j] = -sine


def entry_barrier(f, s, nfac, nst):
    barrier = pltpu.get_barrier_semaphore()
    for k in range(1, nfac):
        pl.semaphore_signal(barrier, inc=1, device_id=(lax.rem(f + k, nfac), s), device_id_type=MESH)
    for k in range(1, nst):
        pl.semaphore_signal(barrier, inc=1, device_id=(f, s ^ k), device_id_type=MESH)
    return barrier


def predict_kernel(
    nfac,
    nst,
    owned,
    strips_ref,
    column_ref,
    m0_ref,
    offsets_ref,
    obs_ref,
    yall_ref,
    obuf_ref,
    cbuf,
    ph,
    osend,
    orecv,
    csend,
    crecv,
    ysend,
    yrecv,
):
    f = lax.axis_index("facet")
    s = lax.axis_index("stokes")
    rows = strips_ref.shape[1]
    steps = obuf_ref.shape[1]
    barrier = entry_barrier(f, s, nfac, nst)
    period = column_ref.shape[0] // 2
    folded = []
    for half in range(2):
        acc = None
        for rep in range(4):
            piece = strips_ref[0, :, pl.ds((half * 4 + rep) * period, period)].astype(jnp.float32)
            acc = piece if acc is None else acc + piece
        folded.append(acc.astype(jnp.bfloat16))
    coeffs = jnp.dot(folded[0], column_ref[:period], preferred_element_type=jnp.float32)
    coeffs += jnp.dot(folded[1], column_ref[period:], preferred_element_type=jnp.float32)
    mine = pl.ds(pl.multiple_of(f * rows, rows), rows)
    cbuf[mine, :] = coeffs.astype(jnp.bfloat16)
    pl.semaphore_wait(barrier, nfac + nst - 2)
    coeff_copies = []
    for k in range(1, nfac):
        copy = pltpu.make_async_remote_copy(
            src_ref=cbuf.at[mine],
            dst_ref=cbuf.at[mine],
            send_sem=csend.at[k - 1],
            recv_sem=crecv.at[k - 1],
            device_id=(lax.rem(f + k, nfac), s),
            device_id_type=MESH,
        )
        copy.start()
        coeff_copies.append(copy)
    obs_copies = []
    for k in range(1, nst):
        peer = s ^ k
        for t in range(steps):
            copy = pltpu.make_async_remote_copy(
                src_ref=obs_ref.at[0, :, :, pl.ds(pl.multiple_of((nst * t + peer) * PAIR, PAIR), PAIR)],
                dst_ref=obuf_ref.at[s, t],
                send_sem=osend.at[k - 1, t],
                recv_sem=orecv.at[k - 1, t],
                device_id=(f, peer),
                device_id_type=MESH,
            )
            copy.start()
            obs_copies.append(copy)
    for t in range(steps):
        obuf_ref[s, t] = obs_ref[0, :, :, pl.ds(pl.multiple_of((nst * t + s) * PAIR, PAIR), PAIR)]
    fill_phases(offsets_ref, f * owned, owned, ph)
    for copy in coeff_copies:
        copy.wait_recv()
    c = cbuf[...].astype(jnp.float32)
    sign = half_sign(c.shape, -1.0)
    swapped = pltpu.roll(c, K, 1) * sign
    tops, bottoms = [], []
    for j in range(owned):
        z = c * ph[j] + swapped * ph[owned + j]
        tops.append(z.astype(jnp.bfloat16))
        bottoms.append((pltpu.roll(z, K, 1) * sign).astype(jnp.bfloat16))
    zz = jnp.concatenate([jnp.concatenate(tops, 1), jnp.concatenate(bottoms, 1)], 0)
    y = jnp.dot(m0_ref[...], zz, preferred_element_type=jnp.float32)
    yall_ref[s] = y.T.astype(jnp.bfloat16)

    def send(slot, bit, index):
        copy = pltpu.make_async_remote_copy(
            src_ref=yall_ref.at[slot],
            dst_ref=yall_ref.at[slot],
            send_sem=ysend.at[index],
            recv_sem=yrecv.at[index],
            device_id=(f, s ^ bit),
            device_id_type=MESH,
        )
        copy.start()
        return copy

    far = send(s, 2, 0)
    near = send(s, 1, 1)
    far.wait_recv()
    relay = send(s ^ 2, 1, 2)
    near.wait_recv()
    relay.wait_recv()
    for copy in obs_copies:
        copy.wait()
    for copy in coeff_copies + [far, near, relay]:
        copy.wait_send()


def visibility_kernel(
    nst, owned, counts_ref, mu_ref, yall_ref, interp_ref, uvw_ref, obs_ref, rbuf_ref, ya_ref, acc
):
    me = lax.axis_index("stokes")
    rbuf_ref[...] = jnp.zeros_like(rbuf_ref)
    acc[...] = jnp.zeros_like(acc)
    width = 2 * K
    for j in range(owned):
        count = counts_ref[j]
        pairs = (count + 1) // 2
        trips = ((pairs - me + nst - 1) // nst + 1) // 2

        def step(t, j=j, count=count):
            pair = nst * t + me
            lanes = pl.ds(pl.multiple_of(pair * PAIR, PAIR), PAIR)
            cells = lax.broadcasted_iota(jnp.int32, (G, PAIR), 0)
            pick_u = jnp.where(cells == uvw_ref[0, j : j + 1, lanes], 1.0, 0.0).astype(jnp.bfloat16)
            pick_w = jnp.where(cells == uvw_ref[1, j : j + 1, lanes], 1.0, 0.0).astype(jnp.bfloat16)
            cosine, sine = turn_of(uvw_ref[2, j : j + 1, lanes], G)
            table = jnp.concatenate(
                [yall_ref[s, j * width : (j + 1) * width, :] for s in range(nst)], 0
            )
            picked = jnp.dot(table, pick_u, preferred_element_type=jnp.float32)
            weights = jnp.dot(interp_ref[...], pick_w, preferred_element_type=jnp.float32)
            w_re, w_im = weights[:K], weights[K:]
            model = []
            for s in range(nst):
                y_re = picked[s * width : s * width + K]
                y_im = picked[s * width + K : (s + 1) * width]
                m_re = jnp.sum(y_re * w_re - y_im * w_im, axis=0, keepdims=True)
                m_im = jnp.sum(y_re * w_im + y_im * w_re, axis=0, keepdims=True)
                model.append(
                    jnp.concatenate([m_re * cosine + m_im * sine, m_im * cosine - m_re * sine], 0)
                )
            block = 2 * pair
            backs = []
            resids = []
            for h in range(2):
                cut = slice(h * BLOCK, (h + 1) * BLOCK)
                mix = [[mu_ref[c, s, j, block + h] for s in range(nst)] for c in range(nst)]
                resid = []
                for c in range(nst):
                    corr = mix[c][0] * model[0][:, cut]
                    for s in range(1, nst):
                        corr += mix[c][s] * model[s][:, cut]
                    value = obs_ref[c, t, j, :, cut] - corr
                    value = jnp.where(block + h < count, value, 0.0)
                    resid.append(value)
                back = []
                for s in range(nst):
                    total = mix[0][s] * resid[0]
                    for c in range(1, nst):
                        total += mix[c][s] * resid[c]
                    back.append(total)
                backs.append(back)
                resids.append(resid)
            for c in range(nst):
                rbuf_ref[c, t, j] = jnp.concatenate([resids[0][c], resids[1][c]], 1)
            terms = []
            for s in range(nst):
                back = jnp.concatenate([backs[0][s], backs[1][s]], 1)
                b_re, b_im = back[0:1], back[1:2]
                g_re = b_re * cosine - b_im * sine
                g_im = b_im * cosine + b_re * sine
                terms.append((g_re * w_re + g_im * w_im).astype(jnp.bfloat16))
                terms.append((g_im * w_re - g_re * w_im).astype(jnp.bfloat16))
            return lax.dot_general(
                jnp.concatenate(terms, 0),
                pick_u,
                (((1,), (1,)), ((), ())),
                preferred_element_type=jnp.float32,
            )

        def two_steps(i, carry):
            acc[j] += step(2 * i) + step(2 * i + 1)
            return carry

        lax.fori_loop(0, trips, two_steps, 0)
        for s in range(nst):
            ya_ref[s, j * width : (j + 1) * width, :] = acc[j, s * width : (s + 1) * width, :].astype(
                jnp.bfloat16
            )


def adjoint_kernel(
    nfac,
    nst,
    owned,
    ya_ref,
    rbuf_ref,
    m2_ref,
    offsets_ref,
    sums_ref,
    rout_ref,
    stage,
    ymid,
    yin,
    part,
    parts_in,
    ph,
    rsend,
    rrecv,
    ysend,
    yrecv,
    psend,
    precv,
):
    f = lax.axis_index("facet")
    s = lax.axis_index("stokes")
    rows = sums_ref.shape[0]
    width = 2 * K
    barrier = entry_barrier(f, s, nfac, nst)
    pl.semaphore_wait(barrier, nfac + nst - 2)

    def send(src, dst, bit, index):
        copy = pltpu.make_async_remote_copy(
            src_ref=src,
            dst_ref=dst,
            send_sem=ysend.at[index],
            recv_sem=yrecv.at[index],
            device_id=(f, s ^ bit),
            device_id_type=MESH,
        )
        copy.start()
        return copy

    first = send(ya_ref.at[s ^ 3], stage.at[0], 1, 0)
    second = send(ya_ref.at[s ^ 1], stage.at[1], 1, 1)
    first.wait_recv()
    ymid[...] = (ya_ref[s ^ 2].astype(jnp.float32) + stage[0].astype(jnp.float32)).astype(jnp.bfloat16)
    third = send(ymid, yin, 2, 2)
    resid_copies = []
    for k in range(1, nst):
        copy = pltpu.make_async_remote_copy(
            src_ref=rbuf_ref.at[s ^ k],
            dst_ref=rout_ref.at[s],
            send_sem=rsend.at[k - 1],
            recv_sem=rrecv.at[k - 1],
            device_id=(f, s ^ k),
            device_id_type=MESH,
        )
        copy.start()
        resid_copies.append(copy)
    rout_ref[s] = rbuf_ref[s]
    fill_phases(offsets_ref, f * owned, owned, ph)
    second.wait_recv()
    own = ya_ref[s].astype(jnp.float32) + stage[1].astype(jnp.float32)
    third.wait_recv()
    own = own + yin[...].astype(jnp.float32)
    turned = []
    for j in range(owned):
        turned.append(own[j * width + K : (j + 1) * width])
        turned.append(-own[j * width : j * width + K])
    rhs = jnp.concatenate([own, jnp.concatenate(turned, 0)], 1).astype(jnp.bfloat16)
    u = lax.dot_general(
        m2_ref[...], rhs, (((1,), (1,)), ((), ())), preferred_element_type=jnp.float32
    )
    partial = None
    for j in range(owned):
        uj = u[:, j * width : (j + 1) * width]
        term = uj * ph[j] + pltpu.roll(uj, K, 1) * half_sign(uj.shape, 1.0) * ph[owned + j]
        partial = term if partial is None else partial + term
    part[...] = partial.astype(jnp.bfloat16)
    part_copies = []
    for k in range(1, nfac):
        peer = lax.rem(f + k, nfac)
        copy = pltpu.make_async_remote_copy(
            src_ref=part.at[pl.ds(pl.multiple_of(peer * rows, rows), rows)],
            dst_ref=parts_in.at[k - 1],
            send_sem=psend.at[k - 1],
            recv_sem=precv.at[k - 1],
            device_id=(peer, s),
            device_id_type=MESH,
        )
        copy.start()
        part_copies.append(copy)
    result = part[pl.ds(pl.multiple_of(f * rows, rows), rows), :].astype(jnp.float32)
    for k, copy in enumerate(part_copies):
        copy.wait_recv()
        result += parts_in[k].astype(jnp.float32)
    sums_ref[...] = result.astype(jnp.bfloat16)
    for copy in resid_copies:
        copy.wait()
    for copy in part_copies + [first, second, third]:
        copy.wait_send()


def image_kernel(nst, owned, sums_ref, column_ref, rout_ref, image_ref, resid_ref, buf, sems):
    chunks = 4
    period = column_ref.shape[0] // 2
    size = 2 * period // chunks
    steps = rout_ref.shape[1]
    copies = []
    for i in range(chunks):
        cols = pl.ds(i * size, size)
        image = lax.dot_general(
            sums_ref[...], column_ref[cols, :], (((1,), (1,)), ((), ())), preferred_element_type=jnp.float32
        )
        buf[:, cols] = (8.0 * image).astype(jnp.bfloat16)
        half, offset = divmod(i * size, period)
        for rep in range(4):
            copy = pltpu.make_async_copy(
                buf.at[:, cols],
                image_ref.at[0, :, pl.ds((half * 4 + rep) * period + offset, size)],
                sems.at[i, rep],
            )
            copy.start()
            copies.append(copy)
    for q in range(nst):
        for t in range(steps):
            resid_ref[0, :, :, (nst * t + q) * PAIR : (nst * t + q + 1) * PAIR] = rout_ref[q, t]
    for copy in copies:
        copy.wait()


def body(strips, sub_u, counts, uvw, mueller, observed):
    nfac = lax.axis_size("facet")
    nst = lax.axis_size("stokes")
    rows = strips.shape[1]
    length = strips.shape[2] // 2
    total = rows * nfac
    owned = counts.shape[0]
    visits = uvw.shape[2]
    steps = visits // (PAIR * nst)
    wide = owned * 2 * K
    grant = min(60, 20 + total // 32) * 1024 * 1024 if total > 1024 else 20 * 1024 * 1024
    f32, bf16 = jnp.float32, jnp.bfloat16
    interp = interp_table()
    m0 = lift_table(interp, nfac, rows)
    column = jnp.asarray(column_table(length))
    interp_t = jnp.asarray(np.concatenate([interp.real.T, interp.imag.T], 0).astype(ml_dtypes.bfloat16))
    m0_wide = jnp.asarray(np.concatenate([m0.real, m0.imag], 1).astype(ml_dtypes.bfloat16))
    m0_tall = jnp.asarray(np.concatenate([m0.real.T, m0.imag.T], 1).astype(ml_dtypes.bfloat16))
    vmem = pl.BlockSpec(memory_space=pltpu.VMEM)
    smem = pl.BlockSpec(memory_space=pltpu.SMEM)
    dma = pltpu.SemaphoreType.DMA

    yall, obs = pl.pallas_call(
        functools.partial(predict_kernel, nfac, nst, owned),
        out_shape=(
            jax.ShapeDtypeStruct((nst, wide, G), bf16),
            jax.ShapeDtypeStruct((nst, steps, owned, 2, PAIR), f32),
        ),
        in_specs=[vmem, vmem, vmem, smem, vmem],
        out_specs=(vmem, vmem),
        scratch_shapes=[
            pltpu.VMEM((total, 2 * K), bf16),
            pltpu.VMEM((2 * owned, total, 2 * K), f32),
            dma((nst - 1, steps)),
            dma((nst - 1, steps)),
            dma((nfac - 1,)),
            dma((nfac - 1,)),
            dma((3,)),
            dma((3,)),
        ],
        compiler_params=pltpu.CompilerParams(
            collective_id=0, has_side_effects=True, vmem_limit_bytes=grant
        ),
        name="predict",
    )(strips, column, m0_wide, sub_u, observed)

    rbuf, ya = pl.pallas_call(
        functools.partial(visibility_kernel, nst, owned),
        out_shape=(
            jax.ShapeDtypeStruct((nst, steps, owned, 2, PAIR), f32),
            jax.ShapeDtypeStruct((nst, wide, G), bf16),
        ),
        in_specs=[smem, smem, vmem, vmem, vmem, vmem],
        out_specs=(vmem, vmem),
        scratch_shapes=[pltpu.VMEM((owned, nst * 2 * K, G), f32)],
        compiler_params=pltpu.CompilerParams(vmem_limit_bytes=grant),
        name="visibility",
    )(counts, mueller, yall, interp_t, uvw, obs)

    sums, rout = pl.pallas_call(
        functools.partial(adjoint_kernel, nfac, nst, owned),
        out_shape=(
            jax.ShapeDtypeStruct((rows, 2 * K), bf16),
            jax.ShapeDtypeStruct((nst, steps, owned, 2, PAIR), f32),
        ),
        in_specs=[vmem, vmem, vmem, smem],
        out_specs=(vmem, vmem),
        scratch_shapes=[
            pltpu.VMEM((2, wide, G), bf16),
            pltpu.VMEM((wide, G), bf16),
            pltpu.VMEM((wide, G), bf16),
            pltpu.VMEM((total, 2 * K), bf16),
            pltpu.VMEM((nfac - 1, rows, 2 * K), bf16),
            pltpu.VMEM((2 * owned, total, 2 * K), f32),
            dma((nst - 1,)),
            dma((nst - 1,)),
            dma((3,)),
            dma((3,)),
            dma((nfac - 1,)),
            dma((nfac - 1,)),
        ],
        compiler_params=pltpu.CompilerParams(
            collective_id=1, has_side_effects=True, vmem_limit_bytes=grant
        ),
        name="adjoint",
    )(ya, rbuf, m0_tall, sub_u)

    return pl.pallas_call(
        functools.partial(image_kernel, nst, owned),
        out_shape=(
            jax.ShapeDtypeStruct((1, rows, 2 * length), bf16),
            jax.ShapeDtypeStruct((1, owned, 2, visits), f32),
        ),
        in_specs=[vmem] * 3,
        out_specs=(pl.BlockSpec(memory_space=pl.ANY), vmem),
        scratch_shapes=[pltpu.VMEM((rows, length // 2), bf16), dma((4, 4))],
        compiler_params=pltpu.CompilerParams(vmem_limit_bytes=grant),
        name="image",
    )(sums, column, rout)


def solution(mesh):
    placed = (
        P("stokes", "facet", None),
        P(),
        P("facet"),
        P(None, "facet", None),
        P(None, None, "facet", None),
        P("stokes", "facet", None, None),
    )
    return jax.shard_map(
        body,
        mesh=mesh,
        in_specs=placed,
        out_specs=(P("stokes", "facet", None), P("stokes", "facet", None, None)),
        check_vma=False,
    )
```

```python
import functools
import math

import jax
import jax.numpy as jnp
import ml_dtypes
import numpy as np
from jax import lax
from jax.experimental import pallas as pl
from jax.experimental.pallas import tpu as pltpu
from jax.sharding import PartitionSpec as P

K = 64
G = 256
BLOCK = 128
PAIR = 2 * BLOCK
MESH = pl.DeviceIdType.MESH


def unit(phase, period):
    angle = phase.astype(np.float64) * (2.0 * math.pi / period)
    return np.cos(angle) + 1j * np.sin(angle)


def column_table(length):
    period = length // 4
    lpos = np.arange(period, dtype=np.int64)[:, None]
    cpos = np.arange(K, dtype=np.int64)[None, :]
    table = unit(-(4 * cpos * lpos % length), length) / math.sqrt(length)
    re, im = table.real, table.imag
    return np.concatenate([np.concatenate([re, im], 1), np.concatenate([-im, re], 1)], 0).astype(
        ml_dtypes.bfloat16
    )


def interp_table():
    upos = np.arange(G, dtype=np.int64)[:, None, None]
    kpos = np.arange(K, dtype=np.int64)[None, :, None]
    mpos = np.arange(K, dtype=np.int64)[None, None, :] - K // 2
    return unit(mpos * (upos - 4 * kpos) % G, G).sum(2) / (2.0 * K)


def lift_table(interp, nfac, rows):
    total = nfac * rows
    upos = np.arange(G, dtype=np.int64)[:, None]
    kpos = np.arange(K, dtype=np.int64)
    blocks = []
    for f in range(nfac):
        centre = f * rows + rows // 2
        e = interp * unit(4 * kpos[None, :] * centre % total - upos * centre % total, total)
        rpos = f * rows + np.arange(rows, dtype=np.int64)
        fourier = unit(-(4 * kpos[:, None] * rpos[None, :] % total), total) / math.sqrt(total)
        blocks.append(e @ fourier)
    return np.concatenate(blocks, 1)


def turn_of(n, period):
    fraction = n.astype(jnp.float32) * (4.0 / period)
    quarter = (fraction + 0.5).astype(jnp.int32)
    angle = (fraction - quarter.astype(jnp.float32)) * (0.5 * math.pi)
    x2 = angle * angle
    sin = angle * (1.0 + x2 * (-1.0 / 6 + x2 * (1.0 / 120 + x2 * (-1.0 / 5040 + x2 / 362880.0))))
    cos = 1.0 + x2 * (-0.5 + x2 * (1.0 / 24 + x2 * (-1.0 / 720 + x2 / 40320.0)))
    odd = (quarter & 1) == 1
    base_c = jnp.where(odd, sin, cos)
    base_s = jnp.where(odd, cos, sin)
    q = quarter & 3
    cosine = jnp.where((q == 1) | (q == 2), -base_c, base_c)
    sine = jnp.where(q >= 2, -base_s, base_s)
    return cosine, sine


def half_sign(shape, first):
    lane = lax.broadcasted_iota(jnp.int32, shape, 1)
    return jnp.where(lane < K, first, -first).astype(jnp.float32)


def fill_phases(offsets_ref, first, owned, ph):
    total = ph.shape[1]
    rpos = lax.broadcasted_iota(jnp.int32, ph.shape[1:], 0)
    for j in range(owned):
        product = rpos * offsets_ref[first + j]
        phase = product & (total - 1) if total & (total - 1) == 0 else lax.rem(product, total)
        cosine, sine = turn_of(phase, total)
        ph[j] = cosine
        ph[owned + j] = -sine


def entry_barrier(f, s, nfac, nst):
    barrier = pltpu.get_barrier_semaphore()
    for k in range(1, nfac):
        pl.semaphore_signal(barrier, inc=1, device_id=(lax.rem(f + k, nfac), s), device_id_type=MESH)
    for k in range(1, nst):
        pl.semaphore_signal(barrier, inc=1, device_id=(f, s ^ k), device_id_type=MESH)
    return barrier


def predict_kernel(
    nfac,
    nst,
    owned,
    strips_hbm,
    column_hbm,
    m0_hbm,
    offsets_ref,
    obs_hbm,
    yall_ref,
    obuf_ref,
    ph,
    strips_ref,
    column_ref,
    m0_ref,
    cbuf,
    lsem,
    osem,
    osend,
    orecv,
    csend,
    crecv,
    ysend,
    yrecv,
):
    f = lax.axis_index("facet")
    s = lax.axis_index("stokes")
    rows = strips_ref.shape[0]
    steps = obuf_ref.shape[1]
    period = column_ref.shape[0] // 2
    loads = []
    for half in range(2):
        cols = pl.ds(half * 4 * period, 4 * period)
        cells = pl.ds(half * period, period)
        pair = (
            pltpu.make_async_copy(strips_hbm.at[0, :, cols], strips_ref.at[:, cols], lsem.at[2 * half]),
            pltpu.make_async_copy(column_hbm.at[cells], column_ref.at[cells], lsem.at[2 * half + 1]),
        )
        for copy in pair:
            copy.start()
        loads.append(pair)
    load_m0 = pltpu.make_async_copy(m0_hbm, m0_ref, lsem.at[4])
    load_m0.start()

    def seen_by(q, t):
        return obs_hbm.at[0, :, :, pl.ds(pl.multiple_of((nst * t + q) * PAIR, PAIR), PAIR)]

    own_obs = [
        pltpu.make_async_copy(seen_by(s, t), obuf_ref.at[s, t], osem.at[t]) for t in range(steps)
    ]
    for copy in own_obs:
        copy.start()
    barrier = entry_barrier(f, s, nfac, nst)
    coeffs = None
    for half in range(2):
        for copy in loads[half]:
            copy.wait()
        total = None
        for rep in range(4):
            piece = strips_ref[:, pl.ds((half * 4 + rep) * period, period)].astype(jnp.float32)
            total = piece if total is None else total + piece
        term = jnp.dot(
            total.astype(jnp.bfloat16),
            column_ref[pl.ds(half * period, period)],
            preferred_element_type=jnp.float32,
        )
        coeffs = term if coeffs is None else coeffs + term

    def rows_of(owner):
        return pl.ds(pl.multiple_of(owner * rows, rows), rows)

    cbuf[s, rows_of(f), :] = coeffs.astype(jnp.bfloat16)
    pl.semaphore_wait(barrier, nfac + nst - 2)
    started = []

    def push(plane, owner, device, send_sem, recv_sem):
        copy = pltpu.make_async_remote_copy(
            src_ref=cbuf.at[plane, rows_of(owner)],
            dst_ref=cbuf.at[plane, rows_of(owner)],
            send_sem=send_sem,
            recv_sem=recv_sem,
            device_id=device,
            device_id_type=MESH,
        )
        copy.start()
        started.append(copy)
        return copy

    coeff_copies = [None] * nfac
    for k in range(nfac - 1, 0, -1):
        coeff_copies[k] = push(s, f, (f ^ k, s), csend.at[k - 1], crecv.at[k - 1])
    far, near, relay = [], [], []

    def forward(k):
        far.append(push(s, f ^ k, (f, s ^ 2), ysend.at[0, k], yrecv.at[0, k]))
        near.append(push(s, f ^ k, (f, s ^ 1), ysend.at[1, k], yrecv.at[1, k]))

    forward(0)
    obs_copies = []
    for k in range(1, nst):
        for t in range(steps):
            copy = pltpu.make_async_remote_copy(
                src_ref=seen_by(s ^ k, t),
                dst_ref=obuf_ref.at[s, t],
                send_sem=osend.at[k - 1, t],
                recv_sem=orecv.at[k - 1, t],
                device_id=(f, s ^ k),
                device_id_type=MESH,
            )
            obs_copies.append(copy)
    fill_phases(offsets_ref, f * owned, owned, ph)
    for k in range(1, nfac):
        coeff_copies[k].wait_recv()
        forward(k)
    for copy in obs_copies:
        copy.start()
    load_m0.wait()

    def lift(plane):
        c = cbuf[plane].astype(jnp.float32)
        sign = half_sign(c.shape, -1.0)
        swapped = pltpu.roll(c, K, 1) * sign
        tops, bottoms = [], []
        for j in range(owned):
            z = c * ph[j] + swapped * ph[owned + j]
            tops.append(z.astype(jnp.bfloat16))
            bottoms.append((pltpu.roll(z, K, 1) * sign).astype(jnp.bfloat16))
        zz = jnp.concatenate([jnp.concatenate(tops, 1), jnp.concatenate(bottoms, 1)], 0)
        y = jnp.dot(m0_ref[...], zz, preferred_element_type=jnp.float32)
        yall_ref[plane] = y.T.astype(jnp.bfloat16)

    lift(s)
    for k in range(nfac):
        far[k].wait_recv()
        relay.append(push(s ^ 2, f ^ k, (f, s ^ 1), ysend.at[2, k], yrecv.at[2, k]))
    for copy in near:
        copy.wait_recv()
    lift(s ^ 2)
    lift(s ^ 1)
    for copy in relay:
        copy.wait_recv()
    lift(s ^ 3)
    for copy in own_obs + obs_copies:
        copy.wait()
    for copy in started:
        copy.wait_send()


def visibility_kernel(
    nst, owned, counts_ref, mu_ref, yall_ref, interp_ref, uvw_ref, obs_ref, rbuf_ref, ya_ref, acc
):
    me = lax.axis_index("stokes")
    rbuf_ref[...] = jnp.zeros_like(rbuf_ref)
    acc[...] = jnp.zeros_like(acc)
    width = 2 * K
    for j in range(owned):
        count = counts_ref[j]
        pairs = (count + 1) // 2
        trips = ((pairs - me + nst - 1) // nst + 1) // 2

        def step(t, j=j, count=count):
            pair = nst * t + me
            lanes = pl.ds(pl.multiple_of(pair * PAIR, PAIR), PAIR)
            cells = lax.broadcasted_iota(jnp.int32, (G, PAIR), 0)
            pick_u = jnp.where(cells == uvw_ref[0, j : j + 1, lanes], 1.0, 0.0).astype(jnp.bfloat16)
            pick_w = jnp.where(cells == uvw_ref[1, j : j + 1, lanes], 1.0, 0.0).astype(jnp.bfloat16)
            cosine, sine = turn_of(uvw_ref[2, j : j + 1, lanes], G)
            table = jnp.concatenate(
                [yall_ref[s, j * width : (j + 1) * width, :] for s in range(nst)], 0
            )
            picked = jnp.dot(table, pick_u, preferred_element_type=jnp.float32)
            weights = jnp.dot(interp_ref[...], pick_w, preferred_element_type=jnp.float32)
            w_re, w_im = weights[:K], weights[K:]
            model = []
            for s in range(nst):
                y_re = picked[s * width : s * width + K]
                y_im = picked[s * width + K : (s + 1) * width]
                m_re = jnp.sum(y_re * w_re - y_im * w_im, axis=0, keepdims=True)
                m_im = jnp.sum(y_re * w_im + y_im * w_re, axis=0, keepdims=True)
                model.append(
                    jnp.concatenate([m_re * cosine + m_im * sine, m_im * cosine - m_re * sine], 0)
                )
            block = 2 * pair
            backs = []
            resids = []
            for h in range(2):
                cut = slice(h * BLOCK, (h + 1) * BLOCK)
                mix = [[mu_ref[c, s, j, block + h] for s in range(nst)] for c in range(nst)]
                resid = []
                for c in range(nst):
                    corr = mix[c][0] * model[0][:, cut]
                    for s in range(1, nst):
                        corr += mix[c][s] * model[s][:, cut]
                    value = obs_ref[c, t, j, :, cut] - corr
                    value = jnp.where(block + h < count, value, 0.0)
                    resid.append(value)
                back = []
                for s in range(nst):
                    total = mix[0][s] * resid[0]
                    for c in range(1, nst):
                        total += mix[c][s] * resid[c]
                    back.append(total)
                backs.append(back)
                resids.append(resid)
            for c in range(nst):
                rbuf_ref[c, t, j] = jnp.concatenate([resids[0][c], resids[1][c]], 1)
            terms = []
            for s in range(nst):
                back = jnp.concatenate([backs[0][s], backs[1][s]], 1)
                b_re, b_im = back[0:1], back[1:2]
                g_re = b_re * cosine - b_im * sine
                g_im = b_im * cosine + b_re * sine
                terms.append((g_re * w_re + g_im * w_im).astype(jnp.bfloat16))
                terms.append((g_im * w_re - g_re * w_im).astype(jnp.bfloat16))
            return lax.dot_general(
                jnp.concatenate(terms, 0),
                pick_u,
                (((1,), (1,)), ((), ())),
                preferred_element_type=jnp.float32,
            )

        def two_steps(i, carry):
            acc[j] += step(2 * i) + step(2 * i + 1)
            return carry

        lax.fori_loop(0, trips, two_steps, 0)
        for s in range(nst):
            ya_ref[s, j * width : (j + 1) * width, :] = acc[j, s * width : (s + 1) * width, :].astype(
                jnp.bfloat16
            )


def adjoint_kernel(
    nfac,
    nst,
    owned,
    ya_ref,
    rbuf_ref,
    m2_ref,
    ph,
    sums_ref,
    rout_ref,
    stage,
    ymid,
    yin,
    part,
    parts_in,
    rsend,
    rrecv,
    ysend,
    yrecv,
    psend,
    precv,
):
    f = lax.axis_index("facet")
    s = lax.axis_index("stokes")
    rows = sums_ref.shape[0]
    width = 2 * K
    barrier = entry_barrier(f, s, nfac, nst)
    pl.semaphore_wait(barrier, nfac + nst - 2)

    def send(src, dst, bit, index):
        copy = pltpu.make_async_remote_copy(
            src_ref=src,
            dst_ref=dst,
            send_sem=ysend.at[index],
            recv_sem=yrecv.at[index],
            device_id=(f, s ^ bit),
            device_id_type=MESH,
        )
        copy.start()
        return copy

    first = send(ya_ref.at[s ^ 3], stage.at[0], 1, 0)
    second = send(ya_ref.at[s ^ 1], stage.at[1], 1, 1)
    first.wait_recv()
    ymid[...] = (ya_ref[s ^ 2].astype(jnp.float32) + stage[0].astype(jnp.float32)).astype(jnp.bfloat16)
    third = send(ymid, yin, 2, 2)
    resid_copies = []
    for k in range(1, nst):
        copy = pltpu.make_async_remote_copy(
            src_ref=rbuf_ref.at[s ^ k],
            dst_ref=rout_ref.at[s],
            send_sem=rsend.at[k - 1],
            recv_sem=rrecv.at[k - 1],
            device_id=(f, s ^ k),
            device_id_type=MESH,
        )
        copy.start()
        resid_copies.append(copy)
    rout_ref[s] = rbuf_ref[s]
    second.wait_recv()
    own = ya_ref[s].astype(jnp.float32) + stage[1].astype(jnp.float32)
    third.wait_recv()
    own = own + yin[...].astype(jnp.float32)
    turned = []
    for j in range(owned):
        turned.append(own[j * width + K : (j + 1) * width])
        turned.append(-own[j * width : j * width + K])
    rhs = jnp.concatenate([own, jnp.concatenate(turned, 0)], 1).astype(jnp.bfloat16)
    u = lax.dot_general(
        m2_ref[...], rhs, (((1,), (1,)), ((), ())), preferred_element_type=jnp.float32
    )
    partial = None
    for j in range(owned):
        uj = u[:, j * width : (j + 1) * width]
        term = uj * ph[j] + pltpu.roll(uj, K, 1) * half_sign(uj.shape, 1.0) * ph[owned + j]
        partial = term if partial is None else partial + term
    part[...] = partial.astype(jnp.bfloat16)
    part_copies = []
    for k in range(1, nfac):
        peer = lax.rem(f + k, nfac)
        copy = pltpu.make_async_remote_copy(
            src_ref=part.at[pl.ds(pl.multiple_of(peer * rows, rows), rows)],
            dst_ref=parts_in.at[k - 1],
            send_sem=psend.at[k - 1],
            recv_sem=precv.at[k - 1],
            device_id=(peer, s),
            device_id_type=MESH,
        )
        copy.start()
        part_copies.append(copy)
    result = part[pl.ds(pl.multiple_of(f * rows, rows), rows), :].astype(jnp.float32)
    for k, copy in enumerate(part_copies):
        copy.wait_recv()
        result += parts_in[k].astype(jnp.float32)
    sums_ref[...] = result.astype(jnp.bfloat16)
    for copy in resid_copies:
        copy.wait()
    for copy in part_copies + [first, second, third]:
        copy.wait_send()


def image_kernel(nst, owned, sums_ref, column_ref, rout_ref, image_ref, resid_ref, buf, sems):
    chunks = 4
    period = column_ref.shape[0] // 2
    size = 2 * period // chunks
    steps = rout_ref.shape[1]
    copies = []
    for i in range(chunks):
        cols = pl.ds(i * size, size)
        image = lax.dot_general(
            sums_ref[...], column_ref[cols, :], (((1,), (1,)), ((), ())), preferred_element_type=jnp.float32
        )
        buf[:, cols] = (8.0 * image).astype(jnp.bfloat16)
        half, offset = divmod(i * size, period)
        for rep in range(4):
            copy = pltpu.make_async_copy(
                buf.at[:, cols],
                image_ref.at[0, :, pl.ds((half * 4 + rep) * period + offset, size)],
                sems.at[i, rep],
            )
            copy.start()
            copies.append(copy)
    for q in range(nst):
        for t in range(steps):
            resid_ref[0, :, :, (nst * t + q) * PAIR : (nst * t + q + 1) * PAIR] = rout_ref[q, t]
    for copy in copies:
        copy.wait()


def body(strips, sub_u, counts, uvw, mueller, observed):
    nfac = lax.axis_size("facet")
    nst = lax.axis_size("stokes")
    rows = strips.shape[1]
    length = strips.shape[2] // 2
    total = rows * nfac
    owned = counts.shape[0]
    visits = uvw.shape[2]
    steps = visits // (PAIR * nst)
    wide = owned * 2 * K
    grant = min(60, 20 + total // 32) * 1024 * 1024 if total > 1024 else 20 * 1024 * 1024
    f32, bf16 = jnp.float32, jnp.bfloat16
    interp = interp_table()
    m0 = lift_table(interp, nfac, rows)
    column = jnp.asarray(column_table(length))
    interp_t = jnp.asarray(np.concatenate([interp.real.T, interp.imag.T], 0).astype(ml_dtypes.bfloat16))
    m0_wide = jnp.asarray(np.concatenate([m0.real, m0.imag], 1).astype(ml_dtypes.bfloat16))
    m0_tall = jnp.asarray(np.concatenate([m0.real.T, m0.imag.T], 1).astype(ml_dtypes.bfloat16))
    vmem = pl.BlockSpec(memory_space=pltpu.VMEM)
    hbm = pl.BlockSpec(memory_space=pltpu.HBM)
    smem = pl.BlockSpec(memory_space=pltpu.SMEM)
    dma = pltpu.SemaphoreType.DMA

    def in_hbm(array):
        return pltpu.with_memory_space_constraint(array, pltpu.HBM)

    yall, obs, ph = pl.pallas_call(
        functools.partial(predict_kernel, nfac, nst, owned),
        out_shape=(
            jax.ShapeDtypeStruct((nst, wide, G), bf16),
            jax.ShapeDtypeStruct((nst, steps, owned, 2, PAIR), f32),
            jax.ShapeDtypeStruct((2 * owned, total, 2 * K), f32),
        ),
        in_specs=[hbm, hbm, hbm, smem, hbm],
        out_specs=(vmem, vmem, vmem),
        scratch_shapes=[
            pltpu.VMEM((rows, 2 * length), bf16),
            pltpu.VMEM(column.shape, bf16),
            pltpu.VMEM(m0_wide.shape, bf16),
            pltpu.VMEM((nst, total, 2 * K), bf16),
            dma((5,)),
            dma((steps,)),
            dma((nst - 1, steps)),
            dma((nst - 1, steps)),
            dma((nfac - 1,)),
            dma((nfac - 1,)),
            dma((3, nfac)),
            dma((3, nfac)),
        ],
        compiler_params=pltpu.CompilerParams(
            collective_id=0, has_side_effects=True, vmem_limit_bytes=grant
        ),
        name="predict",
    )(in_hbm(strips), in_hbm(column), in_hbm(m0_wide), in_hbm(sub_u), in_hbm(observed))

    rbuf, ya = pl.pallas_call(
        functools.partial(visibility_kernel, nst, owned),
        out_shape=(
            jax.ShapeDtypeStruct((nst, steps, owned, 2, PAIR), f32),
            jax.ShapeDtypeStruct((nst, wide, G), bf16),
        ),
        in_specs=[smem, smem, vmem, vmem, vmem, vmem],
        out_specs=(vmem, vmem),
        scratch_shapes=[pltpu.VMEM((owned, nst * 2 * K, G), f32)],
        compiler_params=pltpu.CompilerParams(vmem_limit_bytes=grant),
        name="visibility",
    )(counts, mueller, yall, interp_t, uvw, obs)

    sums, rout = pl.pallas_call(
        functools.partial(adjoint_kernel, nfac, nst, owned),
        out_shape=(
            jax.ShapeDtypeStruct((rows, 2 * K), bf16),
            jax.ShapeDtypeStruct((nst, steps, owned, 2, PAIR), f32),
        ),
        in_specs=[vmem] * 4,
        out_specs=(vmem, vmem),
        scratch_shapes=[
            pltpu.VMEM((2, wide, G), bf16),
            pltpu.VMEM((wide, G), bf16),
            pltpu.VMEM((wide, G), bf16),
            pltpu.VMEM((total, 2 * K), bf16),
            pltpu.VMEM((nfac - 1, rows, 2 * K), bf16),
            dma((nst - 1,)),
            dma((nst - 1,)),
            dma((3,)),
            dma((3,)),
            dma((nfac - 1,)),
            dma((nfac - 1,)),
        ],
        compiler_params=pltpu.CompilerParams(
            collective_id=1, has_side_effects=True, vmem_limit_bytes=grant
        ),
        name="adjoint",
    )(ya, rbuf, m0_tall, ph)

    return pl.pallas_call(
        functools.partial(image_kernel, nst, owned),
        out_shape=(
            jax.ShapeDtypeStruct((1, rows, 2 * length), bf16),
            jax.ShapeDtypeStruct((1, owned, 2, visits), f32),
        ),
        in_specs=[vmem] * 3,
        out_specs=(pl.BlockSpec(memory_space=pl.ANY), vmem),
        scratch_shapes=[pltpu.VMEM((rows, length // 2), bf16), dma((4, 4))],
        compiler_params=pltpu.CompilerParams(vmem_limit_bytes=grant),
        name="image",
    )(sums, column, rout)


def solution(mesh):
    placed = (
        P("stokes", "facet", None),
        P(),
        P("facet"),
        P(None, "facet", None),
        P(None, None, "facet", None),
        P("stokes", "facet", None, None),
    )
    return jax.shard_map(
        body,
        mesh=mesh,
        in_specs=placed,
        out_specs=(P("stokes", "facet", None), P("stokes", "facet", None, None)),
        check_vma=False,
    )
```

```python
import functools
import math

import jax
import jax.numpy as jnp
import ml_dtypes
import numpy as np
from jax import lax
from jax.experimental import pallas as pl
from jax.experimental.pallas import tpu as pltpu
from jax.sharding import PartitionSpec as P

K = 64
G = 256
BLOCK = 128
PAIR = 2 * BLOCK
MESH = pl.DeviceIdType.MESH


def unit(phase, period):
    angle = phase.astype(np.float64) * (2.0 * math.pi / period)
    return np.cos(angle) + 1j * np.sin(angle)


def column_table(length):
    period = length // 4
    lpos = np.arange(period, dtype=np.int64)[:, None]
    cpos = np.arange(K, dtype=np.int64)[None, :]
    table = unit(-(4 * cpos * lpos % length), length) / math.sqrt(length)
    re, im = table.real, table.imag
    return np.concatenate([np.concatenate([re, im], 1), np.concatenate([-im, re], 1)], 0).astype(
        ml_dtypes.bfloat16
    )


def interp_table():
    upos = np.arange(G, dtype=np.int64)[:, None, None]
    kpos = np.arange(K, dtype=np.int64)[None, :, None]
    mpos = np.arange(K, dtype=np.int64)[None, None, :] - K // 2
    return unit(mpos * (upos - 4 * kpos) % G, G).sum(2) / (2.0 * K)


def lift_table(interp, nfac, rows):
    total = nfac * rows
    upos = np.arange(G, dtype=np.int64)[:, None]
    kpos = np.arange(K, dtype=np.int64)
    blocks = []
    for f in range(nfac):
        centre = f * rows + rows // 2
        e = interp * unit(4 * kpos[None, :] * centre % total - upos * centre % total, total)
        rpos = f * rows + np.arange(rows, dtype=np.int64)
        fourier = unit(-(4 * kpos[:, None] * rpos[None, :] % total), total) / math.sqrt(total)
        blocks.append(e @ fourier)
    return np.concatenate(blocks, 1)


def turn_of(n, period):
    fraction = n.astype(jnp.float32) * (4.0 / period)
    quarter = (fraction + 0.5).astype(jnp.int32)
    angle = (fraction - quarter.astype(jnp.float32)) * (0.5 * math.pi)
    x2 = angle * angle
    sin = angle * (1.0 + x2 * (-1.0 / 6 + x2 * (1.0 / 120 + x2 * (-1.0 / 5040 + x2 / 362880.0))))
    cos = 1.0 + x2 * (-0.5 + x2 * (1.0 / 24 + x2 * (-1.0 / 720 + x2 / 40320.0)))
    odd = (quarter & 1) == 1
    base_c = jnp.where(odd, sin, cos)
    base_s = jnp.where(odd, cos, sin)
    q = quarter & 3
    cosine = jnp.where((q == 1) | (q == 2), -base_c, base_c)
    sine = jnp.where(q >= 2, -base_s, base_s)
    return cosine, sine


def half_sign(shape, first):
    lane = lax.broadcasted_iota(jnp.int32, shape, 1)
    return jnp.where(lane < K, first, -first).astype(jnp.float32)


def fill_phases(offsets_ref, first, owned, ph):
    total = ph.shape[1]
    rpos = lax.broadcasted_iota(jnp.int32, ph.shape[1:], 0)
    for j in range(owned):
        product = rpos * offsets_ref[first + j]
        phase = product & (total - 1) if total & (total - 1) == 0 else lax.rem(product, total)
        cosine, sine = turn_of(phase, total)
        ph[j] = cosine
        ph[owned + j] = -sine


def entry_barrier(f, s, nfac, nst):
    barrier = pltpu.get_barrier_semaphore()
    for k in range(1, nfac):
        pl.semaphore_signal(barrier, inc=1, device_id=(lax.rem(f + k, nfac), s), device_id_type=MESH)
    for k in range(1, nst):
        pl.semaphore_signal(barrier, inc=1, device_id=(f, s ^ k), device_id_type=MESH)
    return barrier


def predict_kernel(
    nfac,
    nst,
    owned,
    strips_hbm,
    column_hbm,
    m0_hbm,
    offsets_ref,
    obs_hbm,
    yall_ref,
    obuf_ref,
    ph,
    strips_ref,
    column_ref,
    m0_ref,
    cbuf,
    lsem,
    osem,
    osend,
    orecv,
    csend,
    crecv,
    ysend,
    yrecv,
):
    f = lax.axis_index("facet")
    s = lax.axis_index("stokes")
    rows = strips_ref.shape[0]
    steps = obuf_ref.shape[1]
    period = column_ref.shape[0] // 2
    loads = []
    for half in range(2):
        cols = pl.ds(half * 4 * period, 4 * period)
        cells = pl.ds(half * period, period)
        pair = (
            pltpu.make_async_copy(strips_hbm.at[0, :, cols], strips_ref.at[:, cols], lsem.at[2 * half]),
            pltpu.make_async_copy(column_hbm.at[cells], column_ref.at[cells], lsem.at[2 * half + 1]),
        )
        for copy in pair:
            copy.start()
        loads.append(pair)
    load_m0 = pltpu.make_async_copy(m0_hbm, m0_ref, lsem.at[4])
    load_m0.start()

    def seen_by(q, t):
        return obs_hbm.at[0, :, :, pl.ds(pl.multiple_of((nst * t + q) * PAIR, PAIR), PAIR)]

    own_obs = [
        pltpu.make_async_copy(seen_by(s, t), obuf_ref.at[s, t], osem.at[t]) for t in range(steps)
    ]
    for copy in own_obs:
        copy.start()
    barrier = entry_barrier(f, s, nfac, nst)
    coeffs = None
    for half in range(2):
        for copy in loads[half]:
            copy.wait()
        total = None
        for rep in range(4):
            piece = strips_ref[:, pl.ds((half * 4 + rep) * period, period)].astype(jnp.float32)
            total = piece if total is None else total + piece
        term = jnp.dot(
            total.astype(jnp.bfloat16),
            column_ref[pl.ds(half * period, period)],
            preferred_element_type=jnp.float32,
        )
        coeffs = term if coeffs is None else coeffs + term

    def rows_of(owner):
        return pl.ds(pl.multiple_of(owner * rows, rows), rows)

    cbuf[s, rows_of(f), :] = coeffs.astype(jnp.bfloat16)
    pl.semaphore_wait(barrier, nfac + nst - 2)
    started = []

    def push(plane, owner, device, send_sem, recv_sem):
        copy = pltpu.make_async_remote_copy(
            src_ref=cbuf.at[plane, rows_of(owner)],
            dst_ref=cbuf.at[plane, rows_of(owner)],
            send_sem=send_sem,
            recv_sem=recv_sem,
            device_id=device,
            device_id_type=MESH,
        )
        copy.start()
        started.append(copy)
        return copy

    coeff_copies = [None] * nfac
    for k in range(nfac - 1, 0, -1):
        coeff_copies[k] = push(s, f, (f ^ k, s), csend.at[k - 1], crecv.at[k - 1])
    far, near, relay = [], [], []

    def forward(k):
        far.append(push(s, f ^ k, (f, s ^ 2), ysend.at[0, k], yrecv.at[0, k]))
        near.append(push(s, f ^ k, (f, s ^ 1), ysend.at[1, k], yrecv.at[1, k]))

    forward(0)
    obs_copies = []
    for k in range(1, nst):
        for t in range(steps):
            copy = pltpu.make_async_remote_copy(
                src_ref=seen_by(s ^ k, t),
                dst_ref=obuf_ref.at[s, t],
                send_sem=osend.at[k - 1, t],
                recv_sem=orecv.at[k - 1, t],
                device_id=(f, s ^ k),
                device_id_type=MESH,
            )
            obs_copies.append(copy)
    fill_phases(offsets_ref, f * owned, owned, ph)
    for k in range(1, nfac):
        coeff_copies[k].wait_recv()
        forward(k)
    for copy in obs_copies:
        copy.start()
    load_m0.wait()

    def lift(plane):
        c = cbuf[plane].astype(jnp.float32)
        sign = half_sign(c.shape, -1.0)
        swapped = pltpu.roll(c, K, 1) * sign
        tops, bottoms = [], []
        for j in range(owned):
            z = c * ph[j] + swapped * ph[owned + j]
            tops.append(z.astype(jnp.bfloat16))
            bottoms.append((pltpu.roll(z, K, 1) * sign).astype(jnp.bfloat16))
        zz = jnp.concatenate([jnp.concatenate(tops, 1), jnp.concatenate(bottoms, 1)], 0)
        y = jnp.dot(m0_ref[...], zz, preferred_element_type=jnp.float32)
        yall_ref[plane] = y.T.astype(jnp.bfloat16)

    lift(s)
    for k in range(nfac):
        far[k].wait_recv()
        relay.append(push(s ^ 2, f ^ k, (f, s ^ 1), ysend.at[2, k], yrecv.at[2, k]))
    for copy in near:
        copy.wait_recv()
    lift(s ^ 2)
    lift(s ^ 1)
    for copy in relay:
        copy.wait_recv()
    lift(s ^ 3)
    for copy in own_obs + obs_copies:
        copy.wait()
    for copy in started:
        copy.wait_send()


def visibility_kernel(
    nst, owned, counts_ref, mu_ref, yall_ref, interp_ref, uvw_ref, obs_ref, rbuf_ref, ya_ref, acc
):
    me = lax.axis_index("stokes")
    rbuf_ref[...] = jnp.zeros_like(rbuf_ref)
    acc[...] = jnp.zeros_like(acc)
    width = 2 * K
    for j in range(owned):
        count = counts_ref[j]
        pairs = (count + 1) // 2
        trips = ((pairs - me + nst - 1) // nst + 1) // 2

        def step(t, j=j, count=count):
            pair = nst * t + me
            lanes = pl.ds(pl.multiple_of(pair * PAIR, PAIR), PAIR)
            cells = lax.broadcasted_iota(jnp.int32, (G, PAIR), 0)
            pick_u = jnp.where(cells == uvw_ref[0, j : j + 1, lanes], 1.0, 0.0).astype(jnp.bfloat16)
            pick_w = jnp.where(cells == uvw_ref[1, j : j + 1, lanes], 1.0, 0.0).astype(jnp.bfloat16)
            cosine, sine = turn_of(uvw_ref[2, j : j + 1, lanes], G)
            table = jnp.concatenate(
                [yall_ref[s, j * width : (j + 1) * width, :] for s in range(nst)], 0
            )
            picked = jnp.dot(table, pick_u, preferred_element_type=jnp.float32)
            weights = jnp.dot(interp_ref[...], pick_w, preferred_element_type=jnp.float32)
            w_re, w_im = weights[:K], weights[K:]
            model = []
            for s in range(nst):
                y_re = picked[s * width : s * width + K]
                y_im = picked[s * width + K : (s + 1) * width]
                m_re = jnp.sum(y_re * w_re - y_im * w_im, axis=0, keepdims=True)
                m_im = jnp.sum(y_re * w_im + y_im * w_re, axis=0, keepdims=True)
                model.append(
                    jnp.concatenate([m_re * cosine + m_im * sine, m_im * cosine - m_re * sine], 0)
                )
            block = 2 * pair
            backs = []
            resids = []
            for h in range(2):
                cut = slice(h * BLOCK, (h + 1) * BLOCK)
                mix = [[mu_ref[c, s, j, block + h] for s in range(nst)] for c in range(nst)]
                resid = []
                for c in range(nst):
                    corr = mix[c][0] * model[0][:, cut]
                    for s in range(1, nst):
                        corr += mix[c][s] * model[s][:, cut]
                    value = obs_ref[c, t, j, :, cut] - corr
                    value = jnp.where(block + h < count, value, 0.0)
                    resid.append(value)
                back = []
                for s in range(nst):
                    total = mix[0][s] * resid[0]
                    for c in range(1, nst):
                        total += mix[c][s] * resid[c]
                    back.append(total)
                backs.append(back)
                resids.append(resid)
            for c in range(nst):
                rbuf_ref[c, t, j] = jnp.concatenate([resids[0][c], resids[1][c]], 1)
            terms = []
            for s in range(nst):
                back = jnp.concatenate([backs[0][s], backs[1][s]], 1)
                b_re, b_im = back[0:1], back[1:2]
                g_re = b_re * cosine - b_im * sine
                g_im = b_im * cosine + b_re * sine
                terms.append((g_re * w_re + g_im * w_im).astype(jnp.bfloat16))
                terms.append((g_im * w_re - g_re * w_im).astype(jnp.bfloat16))
            return lax.dot_general(
                jnp.concatenate(terms, 0),
                pick_u,
                (((1,), (1,)), ((), ())),
                preferred_element_type=jnp.float32,
            )

        def two_steps(i, carry):
            acc[j] += step(2 * i) + step(2 * i + 1)
            return carry

        lax.fori_loop(0, trips, two_steps, 0)
        for s in range(nst):
            ya_ref[s, j * width : (j + 1) * width, :] = acc[j, s * width : (s + 1) * width, :].astype(
                jnp.bfloat16
            )


def adjoint_kernel(
    nfac,
    nst,
    owned,
    ya_ref,
    rbuf_ref,
    m2_ref,
    ph,
    sums_ref,
    rout_ref,
    part,
    stage,
    ymid,
    yin,
    psum,
    parts_in,
    rsend,
    rrecv,
    xsend,
    xrecv,
    ysend,
    yrecv,
    psend,
    precv,
):
    f = lax.axis_index("facet")
    s = lax.axis_index("stokes")
    rows = sums_ref.shape[0]
    width = 2 * K
    barrier = entry_barrier(f, s, nfac, nst)

    def project(plane):
        own = ya_ref[plane]
        turned = []
        for j in range(owned):
            turned.append(own[j * width + K : (j + 1) * width])
            turned.append(-own[j * width : j * width + K])
        rhs = jnp.concatenate([own, jnp.concatenate(turned, 0)], 1)
        u = lax.dot_general(
            m2_ref[...], rhs, (((1,), (1,)), ((), ())), preferred_element_type=jnp.float32
        )
        partial, cross = None, None
        for j in range(owned):
            uj = u[:, j * width : (j + 1) * width]
            straight, crossed = uj * ph[j], pltpu.roll(uj, K, 1) * ph[owned + j]
            partial = straight if partial is None else partial + straight
            cross = crossed if cross is None else cross + crossed
        part[plane] = (partial + cross * half_sign(cross.shape, 1.0)).astype(jnp.bfloat16)

    def exchange(src, dst, send_sem, recv_sem, device):
        copy = pltpu.make_async_remote_copy(
            src_ref=src,
            dst_ref=dst,
            send_sem=send_sem,
            recv_sem=recv_sem,
            device_id=device,
            device_id_type=MESH,
        )
        copy.start()
        return copy

    def rows_of(k):
        return pl.ds(pl.multiple_of((f ^ k) * rows, rows), rows)

    project(s ^ 3)
    pl.semaphore_wait(barrier, nfac + nst - 2)
    first = exchange(part.at[s ^ 3], stage.at[0], xsend.at[0], xrecv.at[0], (f, s ^ 1))
    project(s ^ 2)
    first.wait_recv()
    far_first = list(range(nfac - 1, -1, -1))
    mids = {}
    for k in far_first:
        here = rows_of(k)
        ymid[here, :] = (
            part[s ^ 2, here, :].astype(jnp.float32) + stage[0, here, :].astype(jnp.float32)
        ).astype(jnp.bfloat16)
        mids[k] = exchange(ymid.at[here], yin.at[here], ysend.at[k], yrecv.at[k], (f, s ^ 2))
    project(s ^ 1)
    second = exchange(part.at[s ^ 1], stage.at[1], xsend.at[1], xrecv.at[1], (f, s ^ 1))
    project(s)
    resid_copies = []
    for k in range(1, nst):
        resid_copies.append(
            exchange(
                rbuf_ref.at[s ^ k], rout_ref.at[s], rsend.at[k - 1], rrecv.at[k - 1], (f, s ^ k)
            )
        )
    second.wait_recv()
    part_copies = {}
    result = None
    for k in far_first:
        here = rows_of(k)
        mids[k].wait_recv()
        value = (
            part[s, here, :].astype(jnp.float32)
            + stage[1, here, :].astype(jnp.float32)
            + yin[here, :].astype(jnp.float32)
        )
        if k == 0:
            result = value
        else:
            psum[here, :] = value.astype(jnp.bfloat16)
            part_copies[k] = exchange(
                psum.at[here], parts_in.at[k - 1], psend.at[k - 1], precv.at[k - 1], (f ^ k, s)
            )
    rout_ref[s] = rbuf_ref[s]
    for k in range(1, nfac):
        part_copies[k].wait_recv()
        result += parts_in[k - 1].astype(jnp.float32)
    sums_ref[...] = result.astype(jnp.bfloat16)
    for copy in resid_copies:
        copy.wait()
    for copy in [first, second] + [mids[k] for k in far_first] + list(part_copies.values()):
        copy.wait_send()


def image_kernel(nst, owned, sums_ref, column_ref, rout_ref, image_ref, resid_ref, buf, sems):
    chunks = 4
    period = column_ref.shape[0] // 2
    size = 2 * period // chunks
    steps = rout_ref.shape[1]
    copies = []
    for i in range(chunks):
        cols = pl.ds(i * size, size)
        image = lax.dot_general(
            sums_ref[...], column_ref[cols, :], (((1,), (1,)), ((), ())), preferred_element_type=jnp.float32
        )
        buf[:, cols] = (8.0 * image).astype(jnp.bfloat16)
        half, offset = divmod(i * size, period)
        for rep in range(4):
            copy = pltpu.make_async_copy(
                buf.at[:, cols],
                image_ref.at[0, :, pl.ds((half * 4 + rep) * period + offset, size)],
                sems.at[i, rep],
            )
            copy.start()
            copies.append(copy)
    for q in range(nst):
        for t in range(steps):
            resid_ref[0, :, :, (nst * t + q) * PAIR : (nst * t + q + 1) * PAIR] = rout_ref[q, t]
    for copy in copies:
        copy.wait()


def body(strips, sub_u, counts, uvw, mueller, observed):
    nfac = lax.axis_size("facet")
    nst = lax.axis_size("stokes")
    rows = strips.shape[1]
    length = strips.shape[2] // 2
    total = rows * nfac
    owned = counts.shape[0]
    visits = uvw.shape[2]
    steps = visits // (PAIR * nst)
    wide = owned * 2 * K
    grant = min(60, 20 + total // 32) * 1024 * 1024 if total > 1024 else 20 * 1024 * 1024
    f32, bf16 = jnp.float32, jnp.bfloat16
    interp = interp_table()
    m0 = lift_table(interp, nfac, rows)
    column = jnp.asarray(column_table(length))
    interp_t = jnp.asarray(np.concatenate([interp.real.T, interp.imag.T], 0).astype(ml_dtypes.bfloat16))
    m0_wide = jnp.asarray(np.concatenate([m0.real, m0.imag], 1).astype(ml_dtypes.bfloat16))
    m0_tall = jnp.asarray(np.concatenate([m0.real.T, m0.imag.T], 1).astype(ml_dtypes.bfloat16))
    vmem = pl.BlockSpec(memory_space=pltpu.VMEM)
    hbm = pl.BlockSpec(memory_space=pltpu.HBM)
    smem = pl.BlockSpec(memory_space=pltpu.SMEM)
    dma = pltpu.SemaphoreType.DMA

    def in_hbm(array):
        return pltpu.with_memory_space_constraint(array, pltpu.HBM)

    yall, obs, ph = pl.pallas_call(
        functools.partial(predict_kernel, nfac, nst, owned),
        out_shape=(
            jax.ShapeDtypeStruct((nst, wide, G), bf16),
            jax.ShapeDtypeStruct((nst, steps, owned, 2, PAIR), f32),
            jax.ShapeDtypeStruct((2 * owned, total, 2 * K), f32),
        ),
        in_specs=[hbm, hbm, hbm, smem, hbm],
        out_specs=(vmem, vmem, vmem),
        scratch_shapes=[
            pltpu.VMEM((rows, 2 * length), bf16),
            pltpu.VMEM(column.shape, bf16),
            pltpu.VMEM(m0_wide.shape, bf16),
            pltpu.VMEM((nst, total, 2 * K), bf16),
            dma((5,)),
            dma((steps,)),
            dma((nst - 1, steps)),
            dma((nst - 1, steps)),
            dma((nfac - 1,)),
            dma((nfac - 1,)),
            dma((3, nfac)),
            dma((3, nfac)),
        ],
        compiler_params=pltpu.CompilerParams(
            collective_id=0, has_side_effects=True, vmem_limit_bytes=grant
        ),
        name="predict",
    )(in_hbm(strips), in_hbm(column), in_hbm(m0_wide), in_hbm(sub_u), in_hbm(observed))

    rbuf, ya = pl.pallas_call(
        functools.partial(visibility_kernel, nst, owned),
        out_shape=(
            jax.ShapeDtypeStruct((nst, steps, owned, 2, PAIR), f32),
            jax.ShapeDtypeStruct((nst, wide, G), bf16),
        ),
        in_specs=[smem, smem, vmem, vmem, vmem, vmem],
        out_specs=(vmem, vmem),
        scratch_shapes=[pltpu.VMEM((owned, nst * 2 * K, G), f32)],
        compiler_params=pltpu.CompilerParams(vmem_limit_bytes=grant),
        name="visibility",
    )(counts, mueller, yall, interp_t, uvw, obs)

    sums, rout = pl.pallas_call(
        functools.partial(adjoint_kernel, nfac, nst, owned),
        out_shape=(
            jax.ShapeDtypeStruct((rows, 2 * K), bf16),
            jax.ShapeDtypeStruct((nst, steps, owned, 2, PAIR), f32),
        ),
        in_specs=[vmem] * 4,
        out_specs=(vmem, vmem),
        scratch_shapes=[
            pltpu.VMEM((nst, total, 2 * K), bf16),
            pltpu.VMEM((2, total, 2 * K), bf16),
            pltpu.VMEM((total, 2 * K), bf16),
            pltpu.VMEM((total, 2 * K), bf16),
            pltpu.VMEM((total, 2 * K), bf16),
            pltpu.VMEM((nfac - 1, rows, 2 * K), bf16),
            dma((nst - 1,)),
            dma((nst - 1,)),
            dma((2,)),
            dma((2,)),
            dma((nfac,)),
            dma((nfac,)),
            dma((nfac - 1,)),
            dma((nfac - 1,)),
        ],
        compiler_params=pltpu.CompilerParams(
            collective_id=1, has_side_effects=True, vmem_limit_bytes=grant
        ),
        name="adjoint",
    )(ya, rbuf, m0_tall, ph)

    return pl.pallas_call(
        functools.partial(image_kernel, nst, owned),
        out_shape=(
            jax.ShapeDtypeStruct((1, rows, 2 * length), bf16),
            jax.ShapeDtypeStruct((1, owned, 2, visits), f32),
        ),
        in_specs=[vmem] * 3,
        out_specs=(pl.BlockSpec(memory_space=pl.ANY), vmem),
        scratch_shapes=[pltpu.VMEM((rows, length // 2), bf16), dma((4, 4))],
        compiler_params=pltpu.CompilerParams(vmem_limit_bytes=grant),
        name="image",
    )(sums, column, rout)


def solution(mesh):
    placed = (
        P("stokes", "facet", None),
        P(),
        P("facet"),
        P(None, "facet", None),
        P(None, None, "facet", None),
        P("stokes", "facet", None, None),
    )
    return jax.shard_map(
        body,
        mesh=mesh,
        in_specs=placed,
        out_specs=(P("stokes", "facet", None), P("stokes", "facet", None, None)),
        check_vma=False,
    )
```

```python
import functools
import math

import jax
import jax.numpy as jnp
import ml_dtypes
import numpy as np
from jax import lax
from jax.experimental import pallas as pl
from jax.experimental.pallas import tpu as pltpu
from jax.sharding import PartitionSpec as P

K = 64
G = 256
BLOCK = 128
PAIR = 2 * BLOCK
MESH = pl.DeviceIdType.MESH


def unit(phase, period):
    angle = phase.astype(np.float64) * (2.0 * math.pi / period)
    return np.cos(angle) + 1j * np.sin(angle)


def column_table(length):
    period = length // 4
    lpos = np.arange(period, dtype=np.int64)[:, None]
    cpos = np.arange(K, dtype=np.int64)[None, :]
    table = unit(-(4 * cpos * lpos % length), length) / math.sqrt(length)
    re, im = table.real, table.imag
    return np.concatenate([np.concatenate([re, im], 1), np.concatenate([-im, re], 1)], 0).astype(
        ml_dtypes.bfloat16
    )


def interp_table():
    upos = np.arange(G, dtype=np.int64)[:, None, None]
    kpos = np.arange(K, dtype=np.int64)[None, :, None]
    mpos = np.arange(K, dtype=np.int64)[None, None, :] - K // 2
    return unit(mpos * (upos - 4 * kpos) % G, G).sum(2) / (2.0 * K)


def lift_table(interp, nfac, rows):
    total = nfac * rows
    upos = np.arange(G, dtype=np.int64)[:, None]
    kpos = np.arange(K, dtype=np.int64)
    blocks = []
    for f in range(nfac):
        centre = f * rows + rows // 2
        e = interp * unit(4 * kpos[None, :] * centre % total - upos * centre % total, total)
        rpos = f * rows + np.arange(rows, dtype=np.int64)
        fourier = unit(-(4 * kpos[:, None] * rpos[None, :] % total), total) / math.sqrt(total)
        blocks.append(e @ fourier)
    return np.concatenate(blocks, 1)


def turn_of(n, period):
    fraction = n.astype(jnp.float32) * (4.0 / period)
    quarter = (fraction + 0.5).astype(jnp.int32)
    angle = (fraction - quarter.astype(jnp.float32)) * (0.5 * math.pi)
    x2 = angle * angle
    sin = angle * (1.0 + x2 * (-1.0 / 6 + x2 * (1.0 / 120 + x2 * (-1.0 / 5040 + x2 / 362880.0))))
    cos = 1.0 + x2 * (-0.5 + x2 * (1.0 / 24 + x2 * (-1.0 / 720 + x2 / 40320.0)))
    odd = (quarter & 1) == 1
    base_c = jnp.where(odd, sin, cos)
    base_s = jnp.where(odd, cos, sin)
    q = quarter & 3
    cosine = jnp.where((q == 1) | (q == 2), -base_c, base_c)
    sine = jnp.where(q >= 2, -base_s, base_s)
    return cosine, sine


def half_sign(shape, first):
    lane = lax.broadcasted_iota(jnp.int32, shape, 1)
    return jnp.where(lane < K, first, -first).astype(jnp.float32)


def fill_phases(offsets_ref, first, owned, ph):
    total = ph.shape[1]
    rpos = lax.broadcasted_iota(jnp.int32, ph.shape[1:], 0)
    for j in range(owned):
        product = rpos * offsets_ref[first + j]
        phase = product & (total - 1) if total & (total - 1) == 0 else lax.rem(product, total)
        cosine, sine = turn_of(phase, total)
        ph[j] = cosine
        ph[owned + j] = -sine


def entry_barrier(f, s, nfac, nst):
    barrier = pltpu.get_barrier_semaphore()
    for k in range(1, nfac):
        pl.semaphore_signal(barrier, inc=1, device_id=(lax.rem(f + k, nfac), s), device_id_type=MESH)
    for k in range(1, nst):
        pl.semaphore_signal(barrier, inc=1, device_id=(f, s ^ k), device_id_type=MESH)
    return barrier


def predict_kernel(
    nfac,
    nst,
    owned,
    strips_hbm,
    column_hbm,
    m0_hbm,
    offsets_ref,
    obs_hbm,
    yall_ref,
    obuf_ref,
    ph,
    strips_ref,
    column_ref,
    m0_ref,
    cbuf,
    lsem,
    osem,
    osend,
    orecv,
    csend,
    crecv,
    ysend,
    yrecv,
):
    f = lax.axis_index("facet")
    s = lax.axis_index("stokes")
    rows = strips_ref.shape[0]
    steps = obuf_ref.shape[1]
    period = column_ref.shape[0] // 2
    loads = []
    for half in range(2):
        cols = pl.ds(half * 4 * period, 4 * period)
        cells = pl.ds(half * period, period)
        pair = (
            pltpu.make_async_copy(strips_hbm.at[0, :, cols], strips_ref.at[:, cols], lsem.at[2 * half]),
            pltpu.make_async_copy(column_hbm.at[cells], column_ref.at[cells], lsem.at[2 * half + 1]),
        )
        for copy in pair:
            copy.start()
        loads.append(pair)
    load_m0 = pltpu.make_async_copy(m0_hbm, m0_ref, lsem.at[4])
    load_m0.start()

    def seen_by(q, t):
        return obs_hbm.at[0, :, :, pl.ds(pl.multiple_of((nst * t + q) * PAIR, PAIR), PAIR)]

    own_obs = [
        pltpu.make_async_copy(seen_by(s, t), obuf_ref.at[s, t], osem.at[t]) for t in range(steps)
    ]
    for copy in own_obs:
        copy.start()
    barrier = entry_barrier(f, s, nfac, nst)
    coeffs = None
    for half in range(2):
        for copy in loads[half]:
            copy.wait()
        total = None
        for rep in range(4):
            piece = strips_ref[:, pl.ds((half * 4 + rep) * period, period)].astype(jnp.float32)
            total = piece if total is None else total + piece
        term = jnp.dot(
            total.astype(jnp.bfloat16),
            column_ref[pl.ds(half * period, period)],
            preferred_element_type=jnp.float32,
        )
        coeffs = term if coeffs is None else coeffs + term

    def rows_of(owner):
        return pl.ds(pl.multiple_of(owner * rows, rows), rows)

    cbuf[s, rows_of(f), :] = coeffs.astype(jnp.bfloat16)
    pl.semaphore_wait(barrier, nfac + nst - 2)
    started = []

    def push(plane, owner, device, send_sem, recv_sem):
        copy = pltpu.make_async_remote_copy(
            src_ref=cbuf.at[plane, rows_of(owner)],
            dst_ref=cbuf.at[plane, rows_of(owner)],
            send_sem=send_sem,
            recv_sem=recv_sem,
            device_id=device,
            device_id_type=MESH,
        )
        copy.start()
        started.append(copy)
        return copy

    coeff_copies = [None] * nfac
    for k in range(nfac - 1, 0, -1):
        coeff_copies[k] = push(s, f, (f ^ k, s), csend.at[k - 1], crecv.at[k - 1])
    far, near, relay = [], [], []

    def forward(k):
        far.append(push(s, f ^ k, (f, s ^ 2), ysend.at[0, k], yrecv.at[0, k]))
        near.append(push(s, f ^ k, (f, s ^ 1), ysend.at[1, k], yrecv.at[1, k]))

    forward(0)
    obs_copies = []
    for k in range(1, nst):
        for t in range(steps):
            copy = pltpu.make_async_remote_copy(
                src_ref=seen_by(s ^ k, t),
                dst_ref=obuf_ref.at[s, t],
                send_sem=osend.at[k - 1, t],
                recv_sem=orecv.at[k - 1, t],
                device_id=(f, s ^ k),
                device_id_type=MESH,
            )
            obs_copies.append(copy)
    fill_phases(offsets_ref, f * owned, owned, ph)
    for k in range(1, nfac):
        coeff_copies[k].wait_recv()
        forward(k)
    for copy in obs_copies:
        copy.start()
    load_m0.wait()

    def lift(plane):
        c = cbuf[plane].astype(jnp.float32)
        sign = half_sign(c.shape, -1.0)
        swapped = pltpu.roll(c, K, 1) * sign
        tops, bottoms = [], []
        for j in range(owned):
            z = c * ph[j] + swapped * ph[owned + j]
            tops.append(z.astype(jnp.bfloat16))
            bottoms.append((pltpu.roll(z, K, 1) * sign).astype(jnp.bfloat16))
        zz = jnp.concatenate([jnp.concatenate(tops, 1), jnp.concatenate(bottoms, 1)], 0)
        y = jnp.dot(m0_ref[...], zz, preferred_element_type=jnp.float32)
        yall_ref[plane] = y.T.astype(jnp.bfloat16)

    lift(s)
    for k in range(nfac):
        far[k].wait_recv()
        relay.append(push(s ^ 2, f ^ k, (f, s ^ 1), ysend.at[2, k], yrecv.at[2, k]))
    for copy in near:
        copy.wait_recv()
    lift(s ^ 2)
    lift(s ^ 1)
    for copy in relay:
        copy.wait_recv()
    lift(s ^ 3)
    for copy in own_obs + obs_copies:
        copy.wait()
    for copy in started:
        copy.wait_send()


def visibility_kernel(
    nst, owned, counts_ref, mu_ref, yall_ref, interp_ref, uvw_ref, obs_ref, rbuf_ref, ya_ref, acc
):
    me = lax.axis_index("stokes")
    rbuf_ref[...] = jnp.zeros_like(rbuf_ref)
    acc[...] = jnp.zeros_like(acc)
    width = 2 * K
    for j in range(owned):
        count = counts_ref[j]
        pairs = (count + 1) // 2
        trips = ((pairs - me + nst - 1) // nst + 1) // 2

        def step(t, j=j, count=count):
            pair = nst * t + me
            lanes = pl.ds(pl.multiple_of(pair * PAIR, PAIR), PAIR)
            cells = lax.broadcasted_iota(jnp.int32, (G, PAIR), 0)
            pick_u = jnp.where(cells == uvw_ref[0, j : j + 1, lanes], 1.0, 0.0).astype(jnp.bfloat16)
            pick_w = jnp.where(cells == uvw_ref[1, j : j + 1, lanes], 1.0, 0.0).astype(jnp.bfloat16)
            cosine, sine = turn_of(uvw_ref[2, j : j + 1, lanes], G)
            table = jnp.concatenate(
                [yall_ref[s, j * width : (j + 1) * width, :] for s in range(nst)], 0
            )
            picked = jnp.dot(table, pick_u, preferred_element_type=jnp.float32).astype(jnp.bfloat16)
            weights = jnp.dot(interp_ref[...], pick_w, preferred_element_type=jnp.float32).astype(
                jnp.bfloat16
            )
            w_re, w_im = weights[:K], weights[K:]
            model = []
            for s in range(nst):
                y_re = picked[s * width : s * width + K]
                y_im = picked[s * width + K : (s + 1) * width]
                m_re = jnp.sum((y_re * w_re - y_im * w_im).astype(jnp.float32), axis=0, keepdims=True)
                m_im = jnp.sum((y_re * w_im + y_im * w_re).astype(jnp.float32), axis=0, keepdims=True)
                model.append(
                    jnp.concatenate([m_re * cosine + m_im * sine, m_im * cosine - m_re * sine], 0)
                )
            block = 2 * pair
            backs = []
            resids = []
            for h in range(2):
                cut = slice(h * BLOCK, (h + 1) * BLOCK)
                mix = [[mu_ref[c, s, j, block + h] for s in range(nst)] for c in range(nst)]
                resid = []
                for c in range(nst):
                    corr = mix[c][0] * model[0][:, cut]
                    for s in range(1, nst):
                        corr += mix[c][s] * model[s][:, cut]
                    value = obs_ref[c, t, j, :, cut] - corr
                    value = jnp.where(block + h < count, value, 0.0)
                    resid.append(value)
                back = []
                for s in range(nst):
                    total = mix[0][s] * resid[0]
                    for c in range(1, nst):
                        total += mix[c][s] * resid[c]
                    back.append(total)
                backs.append(back)
                resids.append(resid)
            for c in range(nst):
                rbuf_ref[c, t, j] = jnp.concatenate([resids[0][c], resids[1][c]], 1)
            terms = []
            for s in range(nst):
                back = jnp.concatenate([backs[0][s], backs[1][s]], 1)
                b_re, b_im = back[0:1], back[1:2]
                g_re = (b_re * cosine - b_im * sine).astype(jnp.bfloat16)
                g_im = (b_im * cosine + b_re * sine).astype(jnp.bfloat16)
                terms.append(g_re * w_re + g_im * w_im)
                terms.append(g_im * w_re - g_re * w_im)
            return jnp.concatenate(terms, 0), pick_u

        def two_steps(i, carry):
            terms, picks = zip(step(2 * i), step(2 * i + 1))
            acc[j] += lax.dot_general(
                jnp.concatenate(terms, 1),
                jnp.concatenate(picks, 1),
                (((1,), (1,)), ((), ())),
                preferred_element_type=jnp.float32,
            )
            return carry

        lax.fori_loop(0, trips, two_steps, 0)
        for s in range(nst):
            ya_ref[s, j * width : (j + 1) * width, :] = acc[j, s * width : (s + 1) * width, :].astype(
                jnp.bfloat16
            )


def adjoint_kernel(
    nfac,
    nst,
    owned,
    ya_ref,
    rbuf_ref,
    m2_ref,
    ph,
    sums_ref,
    rout_ref,
    part,
    stage,
    ymid,
    yin,
    psum,
    parts_in,
    rsend,
    rrecv,
    xsend,
    xrecv,
    ysend,
    yrecv,
    psend,
    precv,
):
    f = lax.axis_index("facet")
    s = lax.axis_index("stokes")
    rows = sums_ref.shape[0]
    width = 2 * K
    barrier = entry_barrier(f, s, nfac, nst)

    def project(plane):
        own = ya_ref[plane]
        turned = []
        for j in range(owned):
            turned.append(own[j * width + K : (j + 1) * width])
            turned.append(-own[j * width : j * width + K])
        rhs = jnp.concatenate([own, jnp.concatenate(turned, 0)], 1)
        u = lax.dot_general(
            m2_ref[...], rhs, (((1,), (1,)), ((), ())), preferred_element_type=jnp.float32
        )
        partial, cross = None, None
        for j in range(owned):
            uj = u[:, j * width : (j + 1) * width]
            straight, crossed = uj * ph[j], pltpu.roll(uj, K, 1) * ph[owned + j]
            partial = straight if partial is None else partial + straight
            cross = crossed if cross is None else cross + crossed
        part[plane] = (partial + cross * half_sign(cross.shape, 1.0)).astype(jnp.bfloat16)

    def exchange(src, dst, send_sem, recv_sem, device):
        copy = pltpu.make_async_remote_copy(
            src_ref=src,
            dst_ref=dst,
            send_sem=send_sem,
            recv_sem=recv_sem,
            device_id=device,
            device_id_type=MESH,
        )
        copy.start()
        return copy

    def rows_of(k):
        return pl.ds(pl.multiple_of((f ^ k) * rows, rows), rows)

    project(s ^ 3)
    pl.semaphore_wait(barrier, nfac + nst - 2)
    first = exchange(part.at[s ^ 3], stage.at[0], xsend.at[0], xrecv.at[0], (f, s ^ 1))
    project(s ^ 2)
    first.wait_recv()
    far_first = list(range(nfac - 1, -1, -1))
    mids = {}
    for k in far_first:
        here = rows_of(k)
        ymid[here, :] = (
            part[s ^ 2, here, :].astype(jnp.float32) + stage[0, here, :].astype(jnp.float32)
        ).astype(jnp.bfloat16)
        mids[k] = exchange(ymid.at[here], yin.at[here], ysend.at[k], yrecv.at[k], (f, s ^ 2))
    project(s ^ 1)
    second = exchange(part.at[s ^ 1], stage.at[1], xsend.at[1], xrecv.at[1], (f, s ^ 1))
    project(s)
    resid_copies = []
    for k in range(1, nst):
        resid_copies.append(
            exchange(
                rbuf_ref.at[s ^ k], rout_ref.at[s], rsend.at[k - 1], rrecv.at[k - 1], (f, s ^ k)
            )
        )
    second.wait_recv()
    part_copies = {}
    result = None
    for k in far_first:
        here = rows_of(k)
        mids[k].wait_recv()
        value = (
            part[s, here, :].astype(jnp.float32)
            + stage[1, here, :].astype(jnp.float32)
            + yin[here, :].astype(jnp.float32)
        )
        if k == 0:
            result = value
        else:
            psum[here, :] = value.astype(jnp.bfloat16)
            part_copies[k] = exchange(
                psum.at[here], parts_in.at[k - 1], psend.at[k - 1], precv.at[k - 1], (f ^ k, s)
            )
    rout_ref[s] = rbuf_ref[s]
    for k in range(1, nfac):
        part_copies[k].wait_recv()
        result += parts_in[k - 1].astype(jnp.float32)
    sums_ref[...] = result.astype(jnp.bfloat16)
    for copy in resid_copies:
        copy.wait()
    for copy in [first, second] + [mids[k] for k in far_first] + list(part_copies.values()):
        copy.wait_send()


def image_kernel(nst, owned, sums_ref, column_ref, rout_ref, image_ref, resid_ref, buf, sems):
    chunks = 4
    period = column_ref.shape[0] // 2
    size = 2 * period // chunks
    steps = rout_ref.shape[1]
    copies = []
    for i in range(chunks):
        cols = pl.ds(i * size, size)
        image = lax.dot_general(
            sums_ref[...], column_ref[cols, :], (((1,), (1,)), ((), ())), preferred_element_type=jnp.float32
        )
        buf[:, cols] = (8.0 * image).astype(jnp.bfloat16)
        half, offset = divmod(i * size, period)
        for rep in range(4):
            copy = pltpu.make_async_copy(
                buf.at[:, cols],
                image_ref.at[0, :, pl.ds((half * 4 + rep) * period + offset, size)],
                sems.at[i, rep],
            )
            copy.start()
            copies.append(copy)
    for q in range(nst):
        for t in range(steps):
            resid_ref[0, :, :, (nst * t + q) * PAIR : (nst * t + q + 1) * PAIR] = rout_ref[q, t]
    for copy in copies:
        copy.wait()


def body(strips, sub_u, counts, uvw, mueller, observed):
    nfac = lax.axis_size("facet")
    nst = lax.axis_size("stokes")
    rows = strips.shape[1]
    length = strips.shape[2] // 2
    total = rows * nfac
    owned = counts.shape[0]
    visits = uvw.shape[2]
    steps = visits // (PAIR * nst)
    wide = owned * 2 * K
    grant = min(60, 20 + total // 32) * 1024 * 1024 if total > 1024 else 20 * 1024 * 1024
    f32, bf16 = jnp.float32, jnp.bfloat16
    interp = interp_table()
    m0 = lift_table(interp, nfac, rows)
    column = jnp.asarray(column_table(length))
    interp_t = jnp.asarray(np.concatenate([interp.real.T, interp.imag.T], 0).astype(ml_dtypes.bfloat16))
    m0_wide = jnp.asarray(np.concatenate([m0.real, m0.imag], 1).astype(ml_dtypes.bfloat16))
    m0_tall = jnp.asarray(np.concatenate([m0.real.T, m0.imag.T], 1).astype(ml_dtypes.bfloat16))
    vmem = pl.BlockSpec(memory_space=pltpu.VMEM)
    hbm = pl.BlockSpec(memory_space=pltpu.HBM)
    smem = pl.BlockSpec(memory_space=pltpu.SMEM)
    dma = pltpu.SemaphoreType.DMA

    def in_hbm(array):
        return pltpu.with_memory_space_constraint(array, pltpu.HBM)

    yall, obs, ph = pl.pallas_call(
        functools.partial(predict_kernel, nfac, nst, owned),
        out_shape=(
            jax.ShapeDtypeStruct((nst, wide, G), bf16),
            jax.ShapeDtypeStruct((nst, steps, owned, 2, PAIR), f32),
            jax.ShapeDtypeStruct((2 * owned, total, 2 * K), f32),
        ),
        in_specs=[hbm, hbm, hbm, smem, hbm],
        out_specs=(vmem, vmem, vmem),
        scratch_shapes=[
            pltpu.VMEM((rows, 2 * length), bf16),
            pltpu.VMEM(column.shape, bf16),
            pltpu.VMEM(m0_wide.shape, bf16),
            pltpu.VMEM((nst, total, 2 * K), bf16),
            dma((5,)),
            dma((steps,)),
            dma((nst - 1, steps)),
            dma((nst - 1, steps)),
            dma((nfac - 1,)),
            dma((nfac - 1,)),
            dma((3, nfac)),
            dma((3, nfac)),
        ],
        compiler_params=pltpu.CompilerParams(
            collective_id=0, has_side_effects=True, vmem_limit_bytes=grant
        ),
        name="predict",
    )(in_hbm(strips), in_hbm(column), in_hbm(m0_wide), in_hbm(sub_u), in_hbm(observed))

    rbuf, ya = pl.pallas_call(
        functools.partial(visibility_kernel, nst, owned),
        out_shape=(
            jax.ShapeDtypeStruct((nst, steps, owned, 2, PAIR), f32),
            jax.ShapeDtypeStruct((nst, wide, G), bf16),
        ),
        in_specs=[smem, smem, vmem, vmem, vmem, vmem],
        out_specs=(vmem, vmem),
        scratch_shapes=[pltpu.VMEM((owned, nst * 2 * K, G), f32)],
        compiler_params=pltpu.CompilerParams(vmem_limit_bytes=grant),
        name="visibility",
    )(counts, mueller, yall, interp_t, uvw, obs)

    sums, rout = pl.pallas_call(
        functools.partial(adjoint_kernel, nfac, nst, owned),
        out_shape=(
            jax.ShapeDtypeStruct((rows, 2 * K), bf16),
            jax.ShapeDtypeStruct((nst, steps, owned, 2, PAIR), f32),
        ),
        in_specs=[vmem] * 4,
        out_specs=(vmem, vmem),
        scratch_shapes=[
            pltpu.VMEM((nst, total, 2 * K), bf16),
            pltpu.VMEM((2, total, 2 * K), bf16),
            pltpu.VMEM((total, 2 * K), bf16),
            pltpu.VMEM((total, 2 * K), bf16),
            pltpu.VMEM((total, 2 * K), bf16),
            pltpu.VMEM((nfac - 1, rows, 2 * K), bf16),
            dma((nst - 1,)),
            dma((nst - 1,)),
            dma((2,)),
            dma((2,)),
            dma((nfac,)),
            dma((nfac,)),
            dma((nfac - 1,)),
            dma((nfac - 1,)),
        ],
        compiler_params=pltpu.CompilerParams(
            collective_id=1, has_side_effects=True, vmem_limit_bytes=grant
        ),
        name="adjoint",
    )(ya, rbuf, m0_tall, ph)

    return pl.pallas_call(
        functools.partial(image_kernel, nst, owned),
        out_shape=(
            jax.ShapeDtypeStruct((1, rows, 2 * length), bf16),
            jax.ShapeDtypeStruct((1, owned, 2, visits), f32),
        ),
        in_specs=[vmem] * 3,
        out_specs=(pl.BlockSpec(memory_space=pl.ANY), vmem),
        scratch_shapes=[pltpu.VMEM((rows, length // 2), bf16), dma((4, 4))],
        compiler_params=pltpu.CompilerParams(vmem_limit_bytes=grant),
        name="image",
    )(sums, column, rout)


def solution(mesh):
    placed = (
        P("stokes", "facet", None),
        P(),
        P("facet"),
        P(None, "facet", None),
        P(None, None, "facet", None),
        P("stokes", "facet", None, None),
    )
    return jax.shard_map(
        body,
        mesh=mesh,
        in_specs=placed,
        out_specs=(P("stokes", "facet", None), P("stokes", "facet", None, None)),
        check_vma=False,
    )
```
